512 devices in a mesh: dp: 8 (over x_hi, y), ctx: 64 (over z, x_lo, core).
Axes of the slice: x: 4 (x_hi: 2, x_lo: 2; x = x_hi * 2 + x_lo), y: 4, z: 16, core: 2. Of those that a mesh axis runs over, the one named last changes fastest.
Arguments:
- embeds: bfloat16 [8, 65536, 128], P('dp', 'ctx'), may hold values from -6 to 6
- perturb: bfloat16 [8, 65536, 128], P('dp', 'ctx'), may hold values from -1.5 to 1.5
- cotangent: bfloat16 [8, 65536, 128], P('dp', 'ctx'), may hold values from -6 to 6
- filter_spectrum: float32 [2, 256, 256, 128], P(None, 'ctx'), may hold values from -4.2 to 4.2
- skip_gain: float32 [128], replicated, may hold values from 0.25 to 1.75
Outputs:
- clean_output: bfloat16 [8, 65536, 128], P('dp', 'ctx')
- filter_grad: float32 [2, 256, 256, 128], P(None, 'ctx', 'dp')
The draws below stay inside these ranges and needn't reach their ends.
All inputs are finite; a program needn't handle non-finite values.
Results may differ from the reference program's by a relative error of at most 0.022.
Values may be sent and summed in bfloat16 or wider, within the bound.
A program may use at most 64 MiB of HBM per device.

```python
import jax
import jax.numpy as jnp
from jax import lax

N1 = 256
N2 = 256
CH = 128
BATCH = 8
SEQLEN = 65536


def shard_levels(stream_key, shape, cuts, low, high):
    def one(dim, blocks):
        draws = jax.random.uniform(jax.random.fold_in(jax.random.fold_in(stream_key, 6), dim), (blocks,), jnp.float32, low / len(cuts), high / len(cuts))
        return jnp.repeat(jnp.exp(draws), shape[dim] // blocks).reshape((-1,) + (1,) * (len(shape) - dim - 1))

    gain = one(*cuts[0])
    for cut in cuts[1:]:
        gain = gain * one(*cut)
    return gain


def gaussian(rng, shape, spread, most, shards=(), kind=jnp.bfloat16):
    level = shard_levels(rng, shape, shards, -0.22, 0.18) if shards else 1.0
    array = jax.random.normal(rng, shape, jnp.float32) * spread * level
    return jnp.minimum(jnp.maximum(array, -most), most).astype(kind)


def setup_inputs(seed: int = 0) -> dict:
    seeds = jax.random.split(jax.random.key(seed), 6)
    embeds = gaussian(seeds[0], (BATCH, SEQLEN, CH), 1.0, 6.0, ((0, 8), (1, 64)))
    perturb = gaussian(seeds[1], (BATCH, SEQLEN, CH), 0.25, 1.5, ((0, 8), (1, 64)))
    cotangent = gaussian(seeds[2], (BATCH, SEQLEN, CH), 1.0, 6.0, ((0, 8), (1, 64)))
    filter_spectrum = gaussian(seeds[3], (2, N1, N2, CH), 0.7, 4.2, ((1, 64),), jnp.float32)
    skip_gain = jnp.clip(1.0 + 0.15 * jax.random.normal(seeds[4], (CH,), jnp.float32), 0.25, 1.75)
    return dict(embeds=embeds, perturb=perturb, cotangent=cotangent, filter_spectrum=filter_spectrum, skip_gain=skip_gain)


two_pi = 6.283185307179586
smart_weight = 2.0


def trig_table(period):
    row_ids = jnp.arange(period, dtype=jnp.int32)
    exponent = (row_ids[:, None] * row_ids[None, :]) % period
    phase_angle = exponent.astype(jnp.float32) * (two_pi / period)
    return jnp.cos(phase_angle).astype(jnp.bfloat16), jnp.sin(phase_angle).astype(jnp.bfloat16)


def left_mul(table, values):
    flat = values.reshape(values.shape[0], -1)
    return jnp.dot(table, flat, preferred_element_type=jnp.float32).reshape(values.shape)


def right_mul(values, table):
    return jnp.einsum("knc,mn->kmc", values.astype(jnp.float32), table.astype(jnp.float32))


def reference(embeds, perturb, cotangent, filter_spectrum, skip_gain):
    cos_one, sin_one = trig_table(N1)
    cos_two, sin_two = trig_table(N2)
    k_ids = jnp.arange(N1, dtype=jnp.int32)
    n_ids = jnp.arange(N2, dtype=jnp.int32)
    exponent = (k_ids[:, None] * n_ids[None, :]) % (N1 * N2)
    phase_angle = exponent.astype(jnp.float32) * (two_pi / (N1 * N2))
    tw_cos = jnp.cos(phase_angle)[:, :, None]
    tw_sin = jnp.sin(phase_angle)[:, :, None]
    inv_len = 1.0 / (N1 * N2)
    filter_real = filter_spectrum[0]
    filter_imag = filter_spectrum[1]

    def forward(signal):
        part_real = left_mul(cos_one, signal)
        part_imag = -left_mul(sin_one, signal)
        half_real = (part_real * tw_cos + part_imag * tw_sin).astype(jnp.bfloat16)
        half_imag = (part_imag * tw_cos - part_real * tw_sin).astype(jnp.bfloat16)
        spec_real = right_mul(half_real, cos_two) + right_mul(half_imag, sin_two)
        spec_imag = right_mul(half_imag, cos_two) - right_mul(half_real, sin_two)
        return spec_real, spec_imag

    def filtered_by(spec_real, spec_imag):
        prod_real = (filter_real * spec_real - filter_imag * spec_imag).astype(jnp.bfloat16)
        prod_imag = (filter_real * spec_imag + filter_imag * spec_real).astype(jnp.bfloat16)
        part_real = right_mul(prod_real, cos_two) - right_mul(prod_imag, sin_two)
        part_imag = right_mul(prod_imag, cos_two) + right_mul(prod_real, sin_two)
        half_real = (part_real * tw_cos - part_imag * tw_sin).astype(jnp.bfloat16)
        half_imag = (part_imag * tw_cos + part_real * tw_sin).astype(jnp.bfloat16)
        filtered = ((left_mul(cos_one, half_real) - left_mul(sin_one, half_imag)) * inv_len).astype(jnp.bfloat16)
        return lax.optimization_barrier(filtered).astype(jnp.float32)

    seq_count = embeds.shape[0]
    channels = embeds.shape[2]
    outputs = []
    grad_total = jnp.zeros((2, N1, N2, channels), jnp.float32)
    for seq_index in range(seq_count):
        clean_rows = embeds[seq_index].reshape(N1, N2, channels)
        clean_wide = clean_rows.astype(jnp.float32)
        shifted = (clean_wide + perturb[seq_index].reshape(N1, N2, channels).astype(jnp.float32)).astype(jnp.bfloat16)
        shifted_wide = shifted.astype(jnp.float32)
        clean_real, clean_imag = forward(clean_rows)
        shift_real, shift_imag = forward(shifted)
        conv_clean = filtered_by(clean_real, clean_imag)
        conv_shift = filtered_by(shift_real, shift_imag)
        clean_y = clean_wide * conv_clean + skip_gain * clean_wide
        shifted_y = shifted_wide * conv_shift + skip_gain * shifted_wide
        outputs.append(clean_y.astype(jnp.bfloat16).reshape(N1 * N2, channels))
        smooth_gap = shifted_y - clean_y
        cot_wide = cotangent[seq_index].reshape(N1, N2, channels).astype(jnp.float32)
        err_clean = (clean_wide * (cot_wide - smart_weight * smooth_gap)).astype(jnp.bfloat16)
        err_shift = (shifted_wide * (smart_weight * smooth_gap)).astype(jnp.bfloat16)
        errc_real, errc_imag = forward(err_clean)
        errs_real, errs_imag = forward(err_shift)
        grad_real = ((errc_real * clean_real + errc_imag * clean_imag) + (errs_real * shift_real + errs_imag * shift_imag)) * inv_len
        grad_imag = ((errc_imag * clean_real - errc_real * clean_imag) + (errs_imag * shift_real - errs_real * shift_imag)) * inv_len
        grad_total = grad_total + jnp.stack([grad_real, grad_imag], 0)
    return jnp.stack(outputs, 0), grad_total
```

```python
import numpy as np
import jax
import jax.numpy as jnp
from jax import lax
from jax.sharding import PartitionSpec as P

M1 = 512
M2 = 128
N = M1 * M2
SMART = 2.0
BF = jnp.bfloat16
F32 = jnp.float32


def trig(rows, cols, period):
    turn = (np.arange(rows)[:, None] * np.arange(cols)[None, :]) % period
    angle = turn * (2.0 * np.pi / period)
    return np.cos(angle), np.sin(angle)


def tables():
    c1, s1 = trig(M1, M1, M1)
    tc, ts = trig(M1, M2, N)
    c2, s2 = trig(M2, M2, M2)
    wf = np.block([[c2, s2], [-s2, c2]])
    wi = np.block([[c2, -s2], [s2, c2]])
    return c1, s1, tc, ts, wf, wi


def dot(a, b, ca, cb):
    return lax.dot_general(a, b, (((ca,), (cb,)), ((), ())), preferred_element_type=F32)


def forward(x, tabs):
    c1, s1, tc, ts, wf, wi = tabs
    ar = dot(c1, x, 1, 0)
    ai = -dot(s1, x, 1, 0)
    tr = (ar * tc + ai * ts).astype(BF)
    ti = (ai * tc - ar * ts).astype(BF)
    return dot(wf, jnp.concatenate([tr, ti], 1), 1, 1)


def convolve(spec, fr, fi, tabs):
    c1, s1, tc, ts, wf, wi = tabs
    re, im = spec[:M2], spec[M2:]
    prod = jnp.concatenate([fr * re - fi * im, fr * im + fi * re], 0).astype(BF)
    v = dot(wi, prod, 1, 0)
    vr, vi = v[:M2], v[M2:]
    sr = (vr * tc.T - vi * ts.T).astype(BF)
    si = (vi * tc.T + vr * ts.T).astype(BF)
    return ((dot(c1, sr, 1, 1) - dot(s1, si, 1, 1)) * (1.0 / N)).astype(BF)


def grad_term(err, spec):
    er, ei, re, im = err[:M2], err[M2:], spec[:M2], spec[M2:]
    return jnp.concatenate([er * re + ei * im, ei * re - er * im], 0)


def channel_work(e, s, c, filt, gain, tabs):
    fr, fi = filt[:M2].astype(F32), filt[M2:].astype(F32)
    ce = forward(e, tabs)
    cs = forward(s, tabs)
    ef, sf = e.astype(F32), s.astype(F32)
    ye = ef * convolve(ce, fr, fi, tabs).astype(F32) + gain * ef
    ys = sf * convolve(cs, fr, fi, tabs).astype(F32) + gain * sf
    gap = ys - ye
    ee = (ef * (c.astype(F32) - SMART * gap)).astype(BF)
    es = (sf * (SMART * gap)).astype(BF)
    g = grad_term(forward(ee, tabs), ce) + grad_term(forward(es, tabs), cs)
    return ye.astype(BF), (g * (1.0 / N)).astype(BF)


def a2a(x, axis):
    return lax.all_to_all(x, axis, split_axis=0, concat_axis=0, tiled=True)


def body(embeds, perturb, cotangent, filter_spectrum, skip_gain):
    tabs = tables()
    cast = (BF, BF, F32, F32, BF, BF)
    tabs = tuple(jnp.asarray(t.astype(np.float32)).astype(k) for t, k in zip(tabs, cast))
    d = lax.axis_index("dp")
    q = lax.axis_index("ctx")
    e = embeds[0]
    s = (e.astype(F32) + perturb[0].astype(F32)).astype(BF)
    sig = jnp.stack([e, s, cotangent[0]], 0).reshape(3, 8, 128, 64, 2)
    sig = a2a(sig.transpose(3, 0, 4, 1, 2), "ctx")
    sig = sig.transpose(1, 2, 0, 3, 4).reshape(3, 2, M1, M2)
    part = lax.dynamic_slice_in_dim(filter_spectrum, d * 32, 32, 2).astype(BF)
    part = part.reshape(2, 4, 16, 2, 64, 2).transpose(4, 1, 3, 5, 0, 2).reshape(64, 4, 128)
    part = a2a(part, "ctx").reshape(256, 2, 2, 2, 16).transpose(2, 3, 4, 1, 0).reshape(2, 2, 16, M1)
    filt = lax.all_gather(part, "dp", axis=2).reshape(2, 2 * M2, M1)
    gains = lax.dynamic_slice_in_dim(skip_gain, 2 * q, 2, 0)
    ys, gs = [], []
    for j in range(2):
        y, g = channel_work(sig[0, j], sig[1, j], sig[2, j], filt[j], gains[j], tabs)
        ys.append(y.reshape(64, 8, 128))
        gs.append(g.reshape(2, 8, 16, M1))
    out = a2a(jnp.stack(ys, 1), "ctx")
    out = out.transpose(2, 3, 0, 1).reshape(1, 1024, 128)
    g = a2a(jnp.stack(gs, 0).transpose(2, 0, 1, 3, 4), "dp")
    g = g.astype(F32).sum(0).reshape(2, 2, 16, 2, 256).transpose(4, 3, 0, 1, 2)
    g = a2a(g.reshape(64, 4, 128).astype(BF), "ctx").reshape(64, 4, 2, 2, 2, 16)
    g = g.transpose(4, 1, 5, 2, 0, 3).reshape(2, 4, 32, 128).astype(F32)
    return out, g


def solution(mesh):
    return jax.shard_map(
        body,
        mesh=mesh,
        in_specs=(
            P("dp", "ctx", None),
            P("dp", "ctx", None),
            P("dp", "ctx", None),
            P(None, "ctx", None, None),
            P(),
        ),
        out_specs=(P("dp", "ctx", None), P(None, "ctx", "dp", None)),
        check_vma=False,
    )
```

```python
import numpy as np
import jax
import jax.numpy as jnp
from jax import lax
from jax.experimental import pallas as pl
from jax.experimental.pallas import tpu as pltpu
from jax.sharding import PartitionSpec as P

M1 = 512
M2 = 128
N = M1 * M2
SMART = 2.0
BF = jnp.bfloat16
F32 = jnp.float32
MESH = pl.DeviceIdType.MESH
NC = 64
ND = 8


def trig(rows, cols, period):
    turn = (np.arange(rows)[:, None] * np.arange(cols)[None, :]) % period
    angle = turn * (2.0 * np.pi / period)
    return np.cos(angle), np.sin(angle)


def tables():
    c1, s1 = trig(M1, M1, M1)
    tc, ts = trig(M1, M2, N)
    c2, s2 = trig(M2, M2, M2)
    wf = np.block([[c2, s2], [-s2, c2]])
    wi = np.block([[c2, -s2], [s2, c2]])

    def blocks(t):
        return t.reshape(4, 128, M2).transpose(0, 2, 1)

    values = (c1, s1, tc, ts, blocks(tc), blocks(ts), wf, wi)
    kinds = (BF, BF, F32, F32, F32, F32, BF, BF)
    return [jnp.asarray(v.astype(np.float32)).astype(k) for v, k in zip(values, kinds)]


def nn(a, b):
    return lax.dot_general(a, b, (((1,), (0,)), ((), ())), preferred_element_type=F32)


def nt(a, b):
    return lax.dot_general(a, b, (((1,), (1,)), ((), ())), preferred_element_type=F32)


def half(x, j):
    return x[:, j * 128:(j + 1) * 128]


def kernel(sig, fmsg, gain, *refs):
    tabs_h, refs = refs[:8], refs[8:]
    out, gout = refs[:2]
    (rsig, rf, fpiece, filt, x, spec, y, sre, sim, osend, gacc, gsend, grecv, zsend) = refs[2:16]
    tabs, refs = refs[16:24], refs[24:]
    tsem, ssem, rsem = refs
    c1, s1, tc, ts, tct, tst, wf, wi = tabs
    me = lax.axis_index("ctx")
    mine = lax.axis_index("dp")
    barrier = pltpu.get_barrier_semaphore()

    def peer(a, count, here):
        step = lax.div(a + 1, 2)
        off = jnp.where(lax.rem(a, 2) == 1, step, count - step)
        return lax.rem(here + off, count)

    def greet(axis, count, here):
        def one(a, _):
            pl.semaphore_signal(
                barrier, inc=1, device_id={axis: peer(a, count, here)}, device_id_type=MESH
            )
            return 0

        lax.fori_loop(1, count, one, 0)

    greet("ctx", NC, me)
    greet("dp", ND, mine)
    loads = [pltpu.make_async_copy(h, v, tsem.at[i]) for i, (h, v) in enumerate(zip(tabs_h, tabs))]
    for load in loads:
        load.start()
    pl.semaphore_wait(barrier, NC + ND - 2)

    def scatter(axis, count, here, src, dst, k):
        pltpu.make_async_copy(src(here), dst(here), rsem.at[k]).start()

        def one(a, _):
            to = peer(a, count, here)
            pltpu.make_async_remote_copy(
                src_ref=src(to),
                dst_ref=dst(here),
                send_sem=ssem.at[k],
                recv_sem=rsem.at[k],
                device_id={axis: to},
                device_id_type=MESH,
            ).start()
            return 0

        lax.fori_loop(1, count, one, 0)

    def arrived(ref, k):
        pltpu.make_async_copy(ref, ref, rsem.at[k]).wait()

    def sent(ref, k):
        pltpu.make_async_copy(ref, ref, ssem.at[k]).wait()

    scatter("ctx", NC, me, lambda r: fmsg.at[r], lambda r: rf.at[r], 3)
    for i in range(3):
        scatter("ctx", NC, me, lambda r, i=i: sig.at[i, r], lambda r, i=i: rsig.at[i, r], i)

    arrived(rf, 3)
    ftab = rf[...].astype(F32).reshape(256, 128)
    for hi in range(2):
        turned = ftab[hi * 128:(hi + 1) * 128].T.astype(BF)
        for h in range(2):
            fpiece[2 * h + hi] = turned[h * 64:(h + 1) * 64].reshape(2, 2, 16, 128)
    scatter("dp", ND, mine, lambda d: fpiece, lambda d: filt.at[d], 4)
    for load in loads:
        load.wait()
    gains = jnp.concatenate([gain[0], gain[1]], 1)

    def gather(i, rows16, j):
        return rsig[i, rows16, j].astype(F32).reshape(128, 128)

    def take(i):
        arrived(rsig.at[i], i)

        def one(b, _):
            for j in range(2):
                x[i, pl.ds(b * 128, 128), j * 128:(j + 1) * 128] = gather(
                    i, pl.ds(b * 16, 16), j
                ).astype(BF)
            return 0

        lax.fori_loop(0, 4, one, 0)

    def forward(i, emit):
        def one(b, _):
            rows = pl.ds(b * 128, 128)
            a = nn(c1[rows, :], x[i])
            m = nn(s1[rows, :], x[i])
            co, si = tc[rows, :], ts[rows, :]
            for j in range(2):
                aj, mj = half(a, j), half(m, j)
                t = jnp.concatenate([aj * co - mj * si, -(mj * co + aj * si)], 1).astype(BF)
                emit(b, j, nt(wf[...], t))
            return 0

        lax.fori_loop(0, 4, one, 0)

    def keep(i):
        def emit(b, j, value):
            spec[i, j, b] = value

        return emit

    def convolve(i, emit):
        def one(b, _):
            for j in range(2):
                re, im = spec[i, j, b, :128], spec[i, j, b, 128:]
                fr = filt[:, b, j, 0].reshape(128, 128).astype(F32)
                fi = filt[:, b, j, 1].reshape(128, 128).astype(F32)
                prod = jnp.concatenate([fr * re - fi * im, fr * im + fi * re], 0).astype(BF)
                v = nn(wi[...], prod)
                vr, vi = v[:128], v[128:]
                co, si = tct[b], tst[b]
                lanes = pl.ds(pl.multiple_of(b * 128, 128), 128)
                sre[j * 128:(j + 1) * 128, lanes] = (vr * co - vi * si).astype(BF)
                sim[j * 128:(j + 1) * 128, lanes] = (vi * co + vr * si).astype(BF)
            return 0

        lax.fori_loop(0, 4, one, 0)

        def two(b, _):
            rows = pl.ds(b * 128, 128)
            conv = (nt(c1[rows, :], sre[...]) - nt(s1[rows, :], sim[...])) * (1.0 / N)
            conv = conv.astype(BF).astype(F32)
            wide = x[i, rows].astype(F32)
            emit(b, rows, wide, wide * conv + gains * wide)
            return 0

        lax.fori_loop(0, 4, two, 0)

    def clean(b, rows, wide, value):
        y[rows] = value
        for j in range(2):
            osend[pl.ds(b * 16, 16), j] = half(value, j).reshape(16, 8, 128).astype(BF)

    def shifted(b, rows, wide, value):
        gap = SMART * (value - y[rows])
        y[rows] = gap
        x[2, rows] = (wide * gap).astype(BF)

    def grad_term(err, i, j, b):
        er, ei = err[:128], err[128:]
        re, im = spec[i, j, b, :128], spec[i, j, b, 128:]
        return jnp.concatenate([er * re + ei * im, ei * re - er * im], 0)

    def first(b, j, err):
        gacc[j, b] = grad_term(err, 1, j, b)

    def second(b, j, err):
        g = ((gacc[j, b] + grad_term(err, 0, j, b)) * (1.0 / N)).astype(BF)
        for p in range(2):
            gsend[b, :, j, p] = g[p * 128:(p + 1) * 128].reshape(8, 16, 128)

    take(0)
    forward(0, keep(0))
    arrived(filt, 4)
    convolve(0, clean)
    scatter("ctx", NC, me, lambda r: osend.at[r], lambda r: out.at[r], 5)
    take(1)
    forward(1, keep(1))
    convolve(1, shifted)
    forward(2, first)
    arrived(rsig.at[2], 2)

    def errors(b, _):
        rows = pl.ds(b * 128, 128)
        for j in range(2):
            lanes = slice(j * 128, (j + 1) * 128)
            cot = gather(2, pl.ds(b * 16, 16), j)
            x[2, rows, lanes] = (x[0, rows, lanes].astype(F32) * (cot - y[rows, lanes])).astype(BF)
        return 0

    lax.fori_loop(0, 4, errors, 0)
    forward(2, second)
    scatter("dp", ND, mine, lambda d: gsend.at[:, d], lambda d: grecv.at[d], 6)
    arrived(grecv, 6)
    total = grecv[0].astype(F32)
    for d in range(1, ND):
        total = total + grecv[d].astype(F32)
    total = total.reshape(4, 64, 128)
    for hi in range(2):
        turned = jnp.concatenate([total[hi], total[2 + hi]], 0).T
        zsend[hi * 32:(hi + 1) * 32] = turned.reshape(32, 4, 128).astype(BF)
    scatter("ctx", NC, me, lambda r: zsend.at[r], lambda r: gout.at[r], 7)
    arrived(out, 5)
    arrived(gout, 7)
    for i in range(3):
        sent(rsig.at[i, pl.ds(0, NC - 1)], i)
    sent(rf.at[pl.ds(0, NC - 1)], 3)
    sent(filt.at[pl.ds(0, ND - 1)], 4)
    sent(osend.at[pl.ds(0, NC - 1)], 5)
    sent(grecv.at[pl.ds(0, ND - 1)], 6)
    sent(zsend.at[pl.ds(0, NC - 1)], 7)


def exchange(sig, part, gains):
    tabs = tables()
    vmem = pl.BlockSpec(memory_space=pltpu.VMEM)
    hbm = pl.BlockSpec(memory_space=pl.ANY)
    return pl.pallas_call(
        kernel,
        out_shape=(
            jax.ShapeDtypeStruct((NC, 2, 8, 128), BF),
            jax.ShapeDtypeStruct((NC, 4, 128), BF),
        ),
        in_specs=[vmem, vmem, vmem] + [hbm] * 8,
        out_specs=(hbm, hbm),
        scratch_shapes=[
            pltpu.VMEM((3, NC, 2, 8, 128), BF),
            pltpu.VMEM((NC, 4, 128), BF),
            pltpu.VMEM((4, 2, 2, 16, 128), BF),
            pltpu.VMEM((ND, 4, 2, 2, 16, 128), BF),
            pltpu.VMEM((3, M1, 256), BF),
            pltpu.VMEM((2, 2, 4, 256, 128), F32),
            pltpu.VMEM((M1, 256), F32),
            pltpu.VMEM((256, M1), BF),
            pltpu.VMEM((256, M1), BF),
            pltpu.VMEM((NC, 2, 8, 128), BF),
            pltpu.VMEM((2, 4, 256, 128), F32),
            pltpu.VMEM((4, ND, 2, 2, 16, 128), BF),
            pltpu.VMEM((ND, 4, 2, 2, 16, 128), BF),
            pltpu.VMEM((NC, 4, 128), BF),
        ]
        + [pltpu.VMEM(t.shape, t.dtype) for t in tabs]
        + [
            pltpu.SemaphoreType.DMA((8,)),
            pltpu.SemaphoreType.DMA((8,)),
            pltpu.SemaphoreType.DMA((8,)),
        ],
        compiler_params=pltpu.CompilerParams(
            collective_id=0, has_side_effects=True, vmem_limit_bytes=48 * 1024 * 1024
        ),
    )(sig, part, gains, *tabs)


def body(embeds, perturb, cotangent, filter_spectrum, skip_gain):
    d = lax.axis_index("dp")
    q = lax.axis_index("ctx")
    e = embeds[0]
    s = (e.astype(F32) + perturb[0].astype(F32)).astype(BF)
    sig = jnp.stack([e, s, cotangent[0]], 0).reshape(3, 8, 128, NC, 2).transpose(0, 3, 4, 1, 2)
    part = lax.dynamic_slice_in_dim(filter_spectrum, d * 32, 32, 2).astype(BF)
    part = part.reshape(2, 4, 16, 2, NC, 2).transpose(4, 1, 3, 5, 0, 2).reshape(NC, 4, 128)
    gains = lax.dynamic_slice_in_dim(skip_gain, 2 * q, 2, 0)
    gains = jnp.broadcast_to(gains[:, None, None], (2, 1, 128))
    out, g = exchange(sig, part, gains)
    out = out.transpose(2, 3, 0, 1).reshape(1, 1024, 128)
    g = g.reshape(NC, 4, 2, 2, 2, 16)
    g = g.transpose(4, 1, 5, 2, 0, 3).reshape(2, 4, 32, 128).astype(F32)
    return out, g


def solution(mesh):
    return jax.shard_map(
        body,
        mesh=mesh,
        in_specs=(
            P("dp", "ctx", None),
            P("dp", "ctx", None),
            P("dp", "ctx", None),
            P(None, "ctx", None, None),
            P(),
        ),
        out_specs=(P("dp", "ctx", None), P(None, "ctx", "dp", None)),
        check_vma=False,
    )
```

```python
import numpy as np
import jax
import jax.numpy as jnp
from jax import lax
from jax.experimental import pallas as pl
from jax.experimental.pallas import tpu as pltpu
from jax.sharding import PartitionSpec as P

M1 = 512
M2 = 128
N = M1 * M2
SMART = 2.0
BF = jnp.bfloat16
F32 = jnp.float32
MESH = pl.DeviceIdType.MESH
NC = 64
ND = 8
VMEM_BYTES = 60 * 1024 * 1024


def trig(rows, cols, period):
    turn = (np.arange(rows)[:, None] * np.arange(cols)[None, :]) % period
    angle = turn * (2.0 * np.pi / period)
    return np.cos(angle), np.sin(angle)


def tables():
    c1, s1 = trig(M1, M1, M1)
    tc, ts = trig(M1, M2, N)
    c2, s2 = trig(M2, M2, M2)
    wf = np.block([[c2, s2], [-s2, c2]])
    wi = np.block([[c2, -s2], [s2, c2]])

    def blocks(t):
        return t.reshape(4, 128, M2).transpose(0, 2, 1)

    values = (c1, s1, tc, ts, blocks(tc), blocks(ts), wf, wi)
    kinds = (BF, BF, F32, F32, F32, F32, BF, BF)
    return [jnp.asarray(v.astype(np.float32)).astype(k) for v, k in zip(values, kinds)]


def nn(a, b):
    return lax.dot_general(a, b, (((1,), (0,)), ((), ())), preferred_element_type=F32)


def nt(a, b):
    return lax.dot_general(a, b, (((1,), (1,)), ((), ())), preferred_element_type=F32)


def half(x, j):
    return x[:, j * 128:(j + 1) * 128]


def kernel(emb, per, cot, fil, gain, *refs):
    tabs_h, refs = refs[:8], refs[8:]
    out, gout = refs[:2]
    (sig, fmsg, oraw, graw) = refs[2:6]
    (rsig, rf, fpiece, filt, x, spec, y, sre, sim, osend, gacc, gsend, grecv, zsend) = refs[6:20]
    (ein, pin, cin, fin, stage, small) = refs[20:26]
    tabs, refs = refs[26:34], refs[34:]
    tsem, ssem, rsem = refs
    c1, s1, tc, ts, tct, tst, wf, wi = tabs
    me = lax.axis_index("ctx")
    mine = lax.axis_index("dp")
    inputs = (
        (fil.at[:, :, pl.ds(pl.multiple_of(mine * 32, 32), 32), :], fin),
        (emb.at[0], ein),
        (per.at[0], pin),
        (cot.at[0], cin),
    )
    copies = [pltpu.make_async_copy(h, v, tsem.at[i]) for i, (h, v) in enumerate(inputs)]
    for copy in copies:
        copy.start()
    barrier = pltpu.get_barrier_semaphore()

    def peer(a, count, here):
        a = count - a
        step = lax.div(a + 1, 2)
        off = jnp.where(lax.rem(a, 2) == 1, step, count - step)
        return lax.rem(here + off, count)

    def greet(axis, count, here):
        def one(a, _):
            pl.semaphore_signal(
                barrier, inc=1, device_id={axis: peer(a, count, here)}, device_id_type=MESH
            )
            return 0

        lax.fori_loop(1, count, one, 0)

    greet("ctx", NC, me)
    greet("dp", ND, mine)
    loads = [
        pltpu.make_async_copy(h, v, tsem.at[4 + i]) for i, (h, v) in enumerate(zip(tabs_h, tabs))
    ]
    for load in loads:
        load.start()
    row = lax.broadcasted_iota(jnp.int32, (128, 128), 0)
    col = lax.broadcasted_iota(jnp.int32, (128, 128), 1)
    eye = jnp.where(row == col, 1.0, 0.0).astype(BF)
    picks = [jnp.where(col[:NC] == 2 * row[:NC] + j, 1.0, 0.0).astype(BF) for j in range(2)]

    def pack(i, source):
        for t in range(8):
            stage[:, t, :] = nt(eye, source[t * 128:(t + 1) * 128, :])
        sig[i] = stage[...].astype(BF).reshape(NC, 2, 8, 128)

    def scatter(axis, count, here, src, dst, k):
        pltpu.make_async_copy(src(here), dst(here), rsem.at[k]).start()

        def one(a, _):
            to = peer(a, count, here)
            pltpu.make_async_remote_copy(
                src_ref=src(to),
                dst_ref=dst(here),
                send_sem=ssem.at[k],
                recv_sem=rsem.at[k],
                device_id={axis: to},
                device_id_type=MESH,
            ).start()
            return 0

        lax.fori_loop(1, count, one, 0)

    def arrived(ref, k):
        pltpu.make_async_copy(ref, ref, rsem.at[k]).wait()

    def sent(ref, k):
        pltpu.make_async_copy(ref, ref, ssem.at[k]).wait()

    def gone(i):
        sent(rsig.at[i, pl.ds(0, NC - 1)], i)

    def send(i):
        scatter("ctx", NC, me, lambda r: sig.at[i, r], lambda r: rsig.at[i, r], i)

    with jax.named_scope("pack_filter"):
        copies[0].wait()
        both = jnp.concatenate(picks, 1)
        for i in range(4):
            z = jnp.concatenate(
                [fin[p, i, pl.ds(h, 16, stride=2), :] for h in range(2) for p in range(2)], 0
            ).astype(BF)
            none = jnp.zeros_like(z)
            wide = jnp.concatenate(
                [jnp.concatenate([z, none], 1), jnp.concatenate([none, z], 1)], 0
            )
            small[:, i, :] = nt(both, wide)
        fmsg[...] = small[...].astype(BF)
    with jax.named_scope("pack_embeds"):
        copies[1].wait()
        pack(0, ein)
    with jax.named_scope("greeted"):
        pl.semaphore_wait(barrier, NC + ND - 2)
    with jax.named_scope("send_filter_embeds"):
        scatter("ctx", NC, me, lambda r: fmsg.at[r], lambda r: rf.at[r], 3)
        send(0)
    with jax.named_scope("pack_others"):
        copies[2].wait()
        pin[...] = (ein[...].astype(F32) + pin[...].astype(F32)).astype(BF)
        pack(1, pin)
        copies[3].wait()
        pack(2, cin)
    with jax.named_scope("embeds_sent"):
        gone(0)
    send(1)
    with jax.named_scope("wait_filter"):
        arrived(rf, 3)
    ftab = rf[...].astype(F32).reshape(256, 128)
    for hi in range(2):
        turned = ftab[hi * 128:(hi + 1) * 128].T.astype(BF)
        for j in range(2):
            for h in range(2):
                base = j * 64 + h * 32
                fpiece[2 * h + hi, j] = turned[base:base + 32].reshape(2, 16, 128)
    scatter("dp", ND, mine, lambda d: fpiece, lambda d: filt.at[d], 4)
    for load in loads:
        load.wait()
    lane = lax.broadcasted_iota(jnp.int32, (1, 128), 1)
    gains = jnp.concatenate(
        [
            jnp.broadcast_to(
                jnp.sum(jnp.where(lane == 2 * me + j, gain[...], 0.0), 1, keepdims=True), (1, 128)
            )
            for j in range(2)
        ],
        1,
    )

    def gather(i, rows16, j):
        return rsig[i, rows16, j].astype(F32).reshape(128, 128)

    def take(i):
        arrived(rsig.at[i], i)

        def one(b, _):
            for j in range(2):
                x[i, pl.ds(b * 128, 128), j * 128:(j + 1) * 128] = gather(
                    i, pl.ds(b * 16, 16), j
                ).astype(BF)
            return 0

        lax.fori_loop(0, 4, one, 0)

    def forward(i, emit, done=None):
        def one(b, _):
            rows = pl.ds(b * 128, 128)
            a = nn(c1[rows, :], x[i])
            m = nn(s1[rows, :], x[i])
            co, si = tc[rows, :], ts[rows, :]
            for j in range(2):
                aj, mj = half(a, j), half(m, j)
                t = jnp.concatenate([aj * co - mj * si, -(mj * co + aj * si)], 1).astype(BF)
                emit(b, j, nt(wf[...], t))
            if done is not None:
                done(b)
            return 0

        lax.fori_loop(0, 4, one, 0)

    def keep(i):
        def emit(b, j, value):
            spec[i, j, b] = value

        return emit

    def convolve(i, emit):
        def one(b, _):
            for j in range(2):
                re, im = spec[i, j, b, :128], spec[i, j, b, 128:]
                fr = filt[:, b, j, 0].reshape(128, 128).astype(F32)
                fi = filt[:, b, j, 1].reshape(128, 128).astype(F32)
                prod = jnp.concatenate([fr * re - fi * im, fr * im + fi * re], 0).astype(BF)
                v = nn(wi[...], prod)
                vr, vi = v[:128], v[128:]
                co, si = tct[b], tst[b]
                lanes = pl.ds(pl.multiple_of(b * 128, 128), 128)
                sre[j * 128:(j + 1) * 128, lanes] = (vr * co - vi * si).astype(BF)
                sim[j * 128:(j + 1) * 128, lanes] = (vi * co + vr * si).astype(BF)
            return 0

        lax.fori_loop(0, 4, one, 0)

        def two(b, _):
            rows = pl.ds(b * 128, 128)
            conv = (nt(c1[rows, :], sre[...]) - nt(s1[rows, :], sim[...])) * (1.0 / N)
            conv = conv.astype(BF).astype(F32)
            wide = x[i, rows].astype(F32)
            emit(b, rows, wide, wide * conv + gains * wide)
            return 0

        lax.fori_loop(0, 4, two, 0)

    def clean(b, rows, wide, value):
        y[rows] = value
        for j in range(2):
            osend[pl.ds(b * 16, 16), j] = half(value, j).reshape(16, 8, 128).astype(BF)

    def shifted(b, rows, wide, value):
        gap = SMART * (value - y[rows])
        y[rows] = gap
        x[2, rows] = (wide * gap).astype(BF)

    def grad_term(err, i, j, b):
        er, ei = err[:128], err[128:]
        re, im = spec[i, j, b, :128], spec[i, j, b, 128:]
        return jnp.concatenate([er * re + ei * im, ei * re - er * im], 0)

    def first(b, j, err):
        gacc[j, b] = grad_term(err, 1, j, b)

    def second(b, j, err):
        g = ((gacc[j, b] + grad_term(err, 0, j, b)) * (1.0 / N)).astype(BF)
        for p in range(2):
            gsend[b, :, j, p] = g[p * 128:(p + 1) * 128].reshape(8, 16, 128)

    def spread(b):
        scatter("dp", ND, mine, lambda d: gsend.at[b, d], lambda d: grecv.at[d, b], 6)

    with jax.named_scope("wait_embeds"):
        take(0)
    with jax.named_scope("forward_embeds"):
        forward(0, keep(0))
    with jax.named_scope("shifted_sent"):
        gone(1)
    send(2)
    with jax.named_scope("wait_filter_dp"):
        arrived(filt, 4)
    with jax.named_scope("convolve_embeds"):
        convolve(0, clean)
    with jax.named_scope("wait_shifted"):
        take(1)
    with jax.named_scope("forward_shifted"):
        forward(1, keep(1))
    with jax.named_scope("convolve_shifted"):
        convolve(1, shifted)
    with jax.named_scope("forward_err_shifted"):
        forward(2, first)
    with jax.named_scope("cotangent_sent"):
        gone(2)
    with jax.named_scope("send_out"):
        scatter("ctx", NC, me, lambda r: osend.at[r], lambda r: oraw.at[r], 5)
    with jax.named_scope("wait_cotangent"):
        arrived(rsig.at[2], 2)

    def errors(b, _):
        rows = pl.ds(b * 128, 128)
        for j in range(2):
            lanes = slice(j * 128, (j + 1) * 128)
            cot = gather(2, pl.ds(b * 16, 16), j)
            x[2, rows, lanes] = (x[0, rows, lanes].astype(F32) * (cot - y[rows, lanes])).astype(BF)
        return 0

    with jax.named_scope("errors"):
        lax.fori_loop(0, 4, errors, 0)
        forward(2, second, spread)
    with jax.named_scope("wait_terms"):
        arrived(grecv, 6)
    total = grecv[0].astype(F32)
    for d in range(1, ND):
        total = total + grecv[d].astype(F32)
    for hi in range(2):
        turned = jnp.concatenate(
            [total[2 * h + hi, j].reshape(32, 128) for j in range(2) for h in range(2)], 0
        ).T
        zsend[hi * 32:(hi + 1) * 32] = turned.reshape(32, 4, 128).astype(BF)
    with jax.named_scope("send_gradient"):
        scatter("ctx", NC, me, lambda r: zsend.at[r], lambda r: graw.at[r], 7)
    with jax.named_scope("wait_out"):
        arrived(oraw, 5)
    stage[...] = oraw[...].astype(F32).reshape(128, 8, 128)
    for t in range(8):
        out[0, t * 128:(t + 1) * 128, :] = nt(eye, stage[:, t, :].astype(BF)).astype(BF)
    with jax.named_scope("wait_gradient"):
        arrived(graw, 7)
    small[...] = graw[...].astype(F32)
    for i in range(4):
        turned = small[:, i, :].T.astype(BF)
        res = nn(turned[:64], picks[0]) + nn(turned[64:], picks[1])
        for h in range(2):
            for p in range(2):
                base = h * 32 + p * 16
                gout[p, i, pl.ds(h, 16, stride=2), :] = res[base:base + 16]
    sent(rf.at[pl.ds(0, NC - 1)], 3)
    sent(filt.at[pl.ds(0, ND - 1)], 4)
    sent(osend.at[pl.ds(0, NC - 1)], 5)
    sent(grecv.at[pl.ds(0, ND - 1)], 6)
    sent(zsend.at[pl.ds(0, NC - 1)], 7)


def body(embeds, perturb, cotangent, filter_spectrum, skip_gain):
    tabs = tables()
    vmem = pl.BlockSpec(memory_space=pltpu.VMEM)
    hbm = pl.BlockSpec(memory_space=pltpu.HBM)
    return pl.pallas_call(
        kernel,
        out_shape=(
            jax.ShapeDtypeStruct((1, 1024, 128), BF),
            jax.ShapeDtypeStruct((2, 4, 32, 128), F32),
        ),
        in_specs=[hbm] * 4 + [vmem] + [hbm] * 8,
        out_specs=(vmem, vmem),
        scratch_shapes=[
            pltpu.VMEM((3, NC, 2, 8, 128), BF),
            pltpu.VMEM((NC, 4, 128), BF),
            pltpu.VMEM((NC, 2, 8, 128), BF),
            pltpu.VMEM((NC, 4, 128), BF),
            pltpu.VMEM((3, NC, 2, 8, 128), BF),
            pltpu.VMEM((NC, 4, 128), BF),
            pltpu.VMEM((4, 2, 2, 16, 128), BF),
            pltpu.VMEM((ND, 4, 2, 2, 16, 128), BF),
            pltpu.VMEM((3, M1, 256), BF),
            pltpu.VMEM((2, 2, 4, 256, 128), F32),
            pltpu.VMEM((M1, 256), F32),
            pltpu.VMEM((256, M1), BF),
            pltpu.VMEM((256, M1), BF),
            pltpu.VMEM((NC, 2, 8, 128), BF),
            pltpu.VMEM((2, 4, 256, 128), F32),
            pltpu.VMEM((4, ND, 2, 2, 16, 128), BF),
            pltpu.VMEM((ND, 4, 2, 2, 16, 128), BF),
            pltpu.VMEM((NC, 4, 128), BF),
            pltpu.VMEM((1024, 128), BF),
            pltpu.VMEM((1024, 128), BF),
            pltpu.VMEM((1024, 128), BF),
            pltpu.VMEM((2, 4, 32, 128), F32),
            pltpu.VMEM((128, 8, 128), F32),
            pltpu.VMEM((NC, 4, 128), F32),
        ]
        + [pltpu.VMEM(t.shape, t.dtype) for t in tabs]
        + [
            pltpu.SemaphoreType.DMA((12,)),
            pltpu.SemaphoreType.DMA((8,)),
            pltpu.SemaphoreType.DMA((8,)),
        ],
        compiler_params=pltpu.CompilerParams(
            collective_id=0, has_side_effects=True, vmem_limit_bytes=VMEM_BYTES
        ),
    )(embeds, perturb, cotangent, filter_spectrum, skip_gain.reshape(1, 128), *tabs)


def solution(mesh):
    return jax.shard_map(
        body,
        mesh=mesh,
        in_specs=(
            P("dp", "ctx", None),
            P("dp", "ctx", None),
            P("dp", "ctx", None),
            P(None, "ctx", None, None),
            P(),
        ),
        out_specs=(P("dp", "ctx", None), P(None, "ctx", "dp", None)),
        check_vma=False,
    )
```

```python
import numpy as np
import jax
import jax.numpy as jnp
from jax import lax
from jax.experimental import pallas as pl
from jax.experimental.pallas import tpu as pltpu
from jax.sharding import PartitionSpec as P

M1 = 512
M2 = 128
N = M1 * M2
SMART = 2.0
BF = jnp.bfloat16
F32 = jnp.float32
MESH = pl.DeviceIdType.MESH
NC = 64
ND = 8
GROUP = 2
VMEM_BYTES = 60 * 1024 * 1024


def trig(rows, cols, period):
    turn = (np.arange(rows)[:, None] * np.arange(cols)[None, :]) % period
    angle = turn * (2.0 * np.pi / period)
    return np.cos(angle), np.sin(angle)


def tables():
    c1, s1 = trig(M1, M1, M1)
    tc, ts = trig(M1, M2, N)
    c2, s2 = trig(M2, M2, M2)
    wf = np.block([[c2, s2], [-s2, c2]])
    wi = np.block([[c2, -s2], [s2, c2]])

    def blocks(t):
        return t.reshape(4, 128, M2).transpose(0, 2, 1)

    values = (c1, s1, tc, ts, blocks(tc), blocks(ts), wf, wi)
    kinds = (BF, BF, F32, F32, F32, F32, BF, BF)
    return [jnp.asarray(v.astype(np.float32)).astype(k) for v, k in zip(values, kinds)]


def nn(a, b):
    return lax.dot_general(a, b, (((1,), (0,)), ((), ())), preferred_element_type=F32)


def nt(a, b):
    return lax.dot_general(a, b, (((1,), (1,)), ((), ())), preferred_element_type=F32)


def half(x, j):
    return x[:, j * 128:(j + 1) * 128]


def kernel(emb, per, cot, fil, gain, *refs):
    tabs_h, refs = refs[:8], refs[8:]
    out, gout = refs[:2]
    (sig, fmsg, oraw, graw) = refs[2:6]
    (rsig, rf, fpiece, filt, x, spec, y, sre, sim, osend, gacc, gsend, grecv, zsend) = refs[6:20]
    (ein, pin, cin, fin, stage, small) = refs[20:26]
    tabs, refs = refs[26:34], refs[34:]
    tsem, ssem, rsem = refs
    c1, s1, tc, ts, tct, tst, wf, wi = tabs
    me = lax.axis_index("ctx")
    mine = lax.axis_index("dp")
    inputs = (
        (fil.at[:, :, pl.ds(pl.multiple_of(mine * 32, 32), 32), :], fin),
        (emb.at[0], ein),
        (per.at[0], pin),
        (cot.at[0], cin),
    )
    copies = [pltpu.make_async_copy(h, v, tsem.at[i]) for i, (h, v) in enumerate(inputs)]
    for copy in copies:
        copy.start()
    barrier = pltpu.get_barrier_semaphore()

    def peer(a, count, here):
        back = count - a
        step = (back + 1) // 2
        return (here + jnp.where(back % 2 == 1, step, count - step)) & (count - 1)

    def greet(axis, count, here):
        def one(a, _):
            pl.semaphore_signal(
                barrier, inc=1, device_id={axis: (here + a) & (count - 1)}, device_id_type=MESH
            )
            return 0

        lax.fori_loop(1, count, one, 0)

    greet("ctx", NC, me)
    greet("dp", ND, mine)
    loads = [
        pltpu.make_async_copy(h, v, tsem.at[4 + i]) for i, (h, v) in enumerate(zip(tabs_h, tabs))
    ]
    for load in loads:
        load.start()
    row = lax.broadcasted_iota(jnp.int32, (128, 128), 0)
    col = lax.broadcasted_iota(jnp.int32, (128, 128), 1)
    eye = jnp.where(row == col, 1.0, 0.0).astype(BF)
    picks = [jnp.where(col[:NC] == 2 * row[:NC] + j, 1.0, 0.0).astype(BF) for j in range(2)]

    def pack(i, source):
        for t in range(8):
            stage[:, t, :] = nt(eye, source[t * 128:(t + 1) * 128, :])
        turned = stage[...].astype(BF).reshape(NC, 2, 8, 128)
        for j in range(2):
            sig[i, j] = turned[:, j]

    def scatter(axis, count, here, src, dst, k):
        pltpu.make_async_copy(src(here), dst(here), rsem.at[k]).start()

        def one(a, _):
            to = peer(a, count, here)
            pltpu.make_async_remote_copy(
                src_ref=src(to),
                dst_ref=dst(here),
                send_sem=ssem.at[k],
                recv_sem=rsem.at[k],
                device_id={axis: to},
                device_id_type=MESH,
            ).start()
            return 0

        lax.fori_loop(1, count, one, 0)

    def arrived(ref, k):
        pltpu.make_async_copy(ref, ref, rsem.at[k]).wait()

    def sent(ref, k):
        pltpu.make_async_copy(ref, ref, ssem.at[k]).wait()

    def gone(i, j):
        sent(rsig.at[i, j, pl.ds(0, NC - 1)], 2 * i + j)

    def send(i, j):
        scatter("ctx", NC, me, lambda r: sig.at[i, j, r], lambda r: rsig.at[i, j, r], 2 * i + j)

    with jax.named_scope("pack_filter"):
        copies[0].wait()
        both = jnp.concatenate(picks, 1)
        for i in range(4):
            z = jnp.concatenate(
                [fin[p, i, pl.ds(h, 16, stride=2), :] for h in range(2) for p in range(2)], 0
            ).astype(BF)
            none = jnp.zeros_like(z)
            wide = jnp.concatenate(
                [jnp.concatenate([z, none], 1), jnp.concatenate([none, z], 1)], 0
            )
            small[:, i, :] = nt(both, wide)
        fmsg[...] = small[...].astype(BF)
    with jax.named_scope("pack_embeds"):
        copies[1].wait()
        pack(0, ein)
    with jax.named_scope("greeted"):
        pl.semaphore_wait(barrier, NC + ND - 2)
    with jax.named_scope("send_filter_embeds"):
        scatter("ctx", NC, me, lambda r: fmsg.at[r], lambda r: rf.at[r], 6)
        send(0, 0)
        send(0, 1)
    with jax.named_scope("pack_others"):
        copies[2].wait()
        pin[...] = (ein[...].astype(F32) + pin[...].astype(F32)).astype(BF)
        pack(1, pin)
        copies[3].wait()
        pack(2, cin)
    with jax.named_scope("embeds_sent"):
        gone(0, 0)
    send(1, 0)
    with jax.named_scope("wait_filter"):
        arrived(rf, 6)
    ftab = rf[...].astype(F32).reshape(256, 128)
    for hi in range(2):
        turned = ftab[hi * 128:(hi + 1) * 128].T.astype(BF)
        for j in range(2):
            for h in range(2):
                base = j * 64 + h * 32
                fpiece[2 * h + hi, j] = turned[base:base + 32].reshape(2, 16, 128)
    scatter("dp", ND, mine, lambda d: fpiece, lambda d: filt.at[d], 7)
    with jax.named_scope("embeds_sent_2"):
        gone(0, 1)
    send(1, 1)
    for load in loads:
        load.wait()
    lane = lax.broadcasted_iota(jnp.int32, (1, 128), 1)
    gains = jnp.concatenate(
        [
            jnp.broadcast_to(
                jnp.sum(jnp.where(lane == 2 * me + j, gain[...], 0.0), 1, keepdims=True), (1, 128)
            )
            for j in range(2)
        ],
        1,
    )

    def blocks(step):
        for b in range(4):
            step(b, 0)

    def gather(i, rows16, j):
        return rsig[i, j, rows16].astype(F32).reshape(128, 128)

    def take(i):
        for j in range(2):
            arrived(rsig.at[i, j], 2 * i + j)

        def one(b, _):
            for j in range(2):
                x[i, pl.ds(b * 128, 128), j * 128:(j + 1) * 128] = gather(
                    i, pl.ds(b * 16, 16), j
                ).astype(BF)
            return 0

        blocks(one)

    def forward(i, emit, done=None, js=(0, 1)):
        lanes = slice(js[0] * 128, js[-1] * 128 + 128)

        def one(b, _):
            rows = pl.ds(b * 128, 128)
            a = nn(c1[rows, :], x[i, :, lanes])
            m = nn(s1[rows, :], x[i, :, lanes])
            co, si = tc[rows, :], ts[rows, :]
            for k, j in enumerate(js):
                aj, mj = half(a, k), half(m, k)
                t = jnp.concatenate([aj * co - mj * si, -(mj * co + aj * si)], 1).astype(BF)
                emit(b, j, nt(wf[...], t))
            if done is not None:
                done(b)
            return 0

        blocks(one)

    def keep(i):
        def emit(b, j, value):
            spec[i, j, b] = value

        return emit

    def convolve(i, emit):
        def one(b, _):
            for j in range(2):
                re, im = spec[i, j, b, :128], spec[i, j, b, 128:]
                fr = filt[:, b, j, 0].reshape(128, 128).astype(F32)
                fi = filt[:, b, j, 1].reshape(128, 128).astype(F32)
                prod = jnp.concatenate([fr * re - fi * im, fr * im + fi * re], 0).astype(BF)
                v = nn(wi[...], prod)
                vr, vi = v[:128], v[128:]
                co, si = tct[b], tst[b]
                lanes = pl.ds(pl.multiple_of(b * 128, 128), 128)
                sre[j * 128:(j + 1) * 128, lanes] = (vr * co - vi * si).astype(BF)
                sim[j * 128:(j + 1) * 128, lanes] = (vi * co + vr * si).astype(BF)
            return 0

        blocks(one)

        def two(b, _):
            rows = pl.ds(b * 128, 128)
            conv = (nt(c1[rows, :], sre[...]) - nt(s1[rows, :], sim[...])) * (1.0 / N)
            conv = conv.astype(BF).astype(F32)
            wide = x[i, rows].astype(F32)
            emit(b, rows, wide, wide * conv + gains * wide)
            return 0

        blocks(two)

    def clean(b, rows, wide, value):
        y[rows] = value
        for j in range(2):
            osend[pl.ds(b * 16, 16), j] = half(value, j).reshape(16, 8, 128).astype(BF)

    def shifted(b, rows, wide, value):
        gap = SMART * (value - y[rows])
        y[rows] = gap
        x[2, rows] = (wide * gap).astype(BF)

    def grad_term(err, i, j, b):
        er, ei = err[:128], err[128:]
        re, im = spec[i, j, b, :128], spec[i, j, b, 128:]
        return jnp.concatenate([er * re + ei * im, ei * re - er * im], 0)

    def first(b, j, err):
        gacc[j, b] = grad_term(err, 1, j, b)

    def second(b, j, err):
        g = ((gacc[j, b] + grad_term(err, 0, j, b)) * (1.0 / N)).astype(BF)
        for p in range(2):
            gsend[j, :, b, p] = g[p * 128:(p + 1) * 128].reshape(8, 16, 128)

    def spread(j):
        def done(b):
            if b % GROUP == GROUP - 1:
                rows = pl.ds(b + 1 - GROUP, GROUP)
                scatter(
                    "dp",
                    ND,
                    mine,
                    lambda d: gsend.at[j, d, rows],
                    lambda d: grecv.at[d, j, rows],
                    9,
                )

        return done

    with jax.named_scope("wait_embeds"):
        take(0)
    with jax.named_scope("forward_embeds"):
        forward(0, keep(0))
    with jax.named_scope("shifted_sent"):
        gone(1, 0)
    send(2, 0)
    with jax.named_scope("wait_filter_dp"):
        arrived(filt, 7)
    with jax.named_scope("convolve_embeds"):
        convolve(0, clean)
    with jax.named_scope("shifted_sent_2"):
        gone(1, 1)
    send(2, 1)
    with jax.named_scope("wait_shifted"):
        take(1)
    with jax.named_scope("forward_shifted"):
        forward(1, keep(1))
    with jax.named_scope("convolve_shifted"):
        convolve(1, shifted)
    with jax.named_scope("forward_err_shifted"):
        forward(2, first)
    with jax.named_scope("cotangent_sent"):
        gone(2, 0)
        gone(2, 1)
    with jax.named_scope("send_out"):
        scatter("ctx", NC, me, lambda r: osend.at[r], lambda r: oraw.at[r], 8)

    def errors(j):
        lanes = slice(j * 128, (j + 1) * 128)

        def one(b, _):
            rows = pl.ds(b * 128, 128)
            cot = gather(2, pl.ds(b * 16, 16), j)
            x[2, rows, lanes] = (x[0, rows, lanes].astype(F32) * (cot - y[rows, lanes])).astype(BF)
            return 0

        blocks(one)
        forward(2, second, spread(j), (j,))

    for j in range(2):
        with jax.named_scope("wait_cotangent"):
            arrived(rsig.at[2, j], 4 + j)
        with jax.named_scope("errors"):
            errors(j)
    with jax.named_scope("wait_terms"):
        arrived(grecv, 9)
    total = grecv[0].astype(F32)
    for d in range(1, ND):
        total = total + grecv[d].astype(F32)
    for hi in range(2):
        turned = jnp.concatenate(
            [total[j, 2 * h + hi].reshape(32, 128) for j in range(2) for h in range(2)], 0
        ).T
        zsend[hi * 32:(hi + 1) * 32] = turned.reshape(32, 4, 128).astype(BF)
    with jax.named_scope("send_gradient"):
        scatter("ctx", NC, me, lambda r: zsend.at[r], lambda r: graw.at[r], 10)
    with jax.named_scope("wait_out"):
        arrived(oraw, 8)
    stage[...] = oraw[...].astype(F32).reshape(128, 8, 128)
    for t in range(8):
        out[0, t * 128:(t + 1) * 128, :] = nt(eye, stage[:, t, :].astype(BF)).astype(BF)
    with jax.named_scope("wait_gradient"):
        arrived(graw, 10)
    small[...] = graw[...].astype(F32)
    for i in range(4):
        turned = small[:, i, :].T.astype(BF)
        res = nn(turned[:64], picks[0]) + nn(turned[64:], picks[1])
        for h in range(2):
            for p in range(2):
                base = h * 32 + p * 16
                gout[p, i, pl.ds(h, 16, stride=2), :] = res[base:base + 16]
    sent(rf.at[pl.ds(0, NC - 1)], 6)
    sent(filt.at[pl.ds(0, ND - 1)], 7)
    sent(osend.at[pl.ds(0, NC - 1)], 8)
    sent(grecv.at[pl.ds(0, ND - 1)], 9)
    sent(zsend.at[pl.ds(0, NC - 1)], 10)


def store(clean, grad, clean_out, grad_out, sem):
    copies = [
        pltpu.make_async_copy(clean, clean_out, sem.at[0]),
        pltpu.make_async_copy(grad, grad_out, sem.at[1]),
    ]
    for copy in copies:
        copy.start()
    for copy in copies:
        copy.wait()


def body(embeds, perturb, cotangent, filter_spectrum, skip_gain):
    tabs = tables()
    vmem = pl.BlockSpec(memory_space=pltpu.VMEM)
    hbm = pl.BlockSpec(memory_space=pltpu.HBM)
    hbm_any = pl.BlockSpec(memory_space=pl.ANY)
    results = pl.pallas_call(
        kernel,
        out_shape=(
            jax.ShapeDtypeStruct((1, 1024, 128), BF),
            jax.ShapeDtypeStruct((2, 4, 32, 128), F32),
        ),
        in_specs=[hbm] * 4 + [vmem] + [hbm] * 8,
        out_specs=(vmem, vmem),
        scratch_shapes=[
            pltpu.VMEM((3, 2, NC, 8, 128), BF),
            pltpu.VMEM((NC, 4, 128), BF),
            pltpu.VMEM((NC, 2, 8, 128), BF),
            pltpu.VMEM((NC, 4, 128), BF),
            pltpu.VMEM((3, 2, NC, 8, 128), BF),
            pltpu.VMEM((NC, 4, 128), BF),
            pltpu.VMEM((4, 2, 2, 16, 128), BF),
            pltpu.VMEM((ND, 4, 2, 2, 16, 128), BF),
            pltpu.VMEM((3, M1, 256), BF),
            pltpu.VMEM((2, 2, 4, 256, 128), F32),
            pltpu.VMEM((M1, 256), F32),
            pltpu.VMEM((256, M1), BF),
            pltpu.VMEM((256, M1), BF),
            pltpu.VMEM((NC, 2, 8, 128), BF),
            pltpu.VMEM((2, 4, 256, 128), F32),
            pltpu.VMEM((2, ND, 4, 2, 16, 128), BF),
            pltpu.VMEM((ND, 2, 4, 2, 16, 128), BF),
            pltpu.VMEM((NC, 4, 128), BF),
            pltpu.VMEM((1024, 128), BF),
            pltpu.VMEM((1024, 128), BF),
            pltpu.VMEM((1024, 128), BF),
            pltpu.VMEM((2, 4, 32, 128), F32),
            pltpu.VMEM((128, 8, 128), F32),
            pltpu.VMEM((NC, 4, 128), F32),
        ]
        + [pltpu.VMEM(t.shape, t.dtype) for t in tabs]
        + [
            pltpu.SemaphoreType.DMA((12,)),
            pltpu.SemaphoreType.DMA((11,)),
            pltpu.SemaphoreType.DMA((11,)),
        ],
        compiler_params=pltpu.CompilerParams(
            collective_id=0, has_side_effects=True, vmem_limit_bytes=VMEM_BYTES
        ),
    )(embeds, perturb, cotangent, filter_spectrum, skip_gain.reshape(1, 128), *tabs)
    return pl.pallas_call(
        store,
        out_shape=[jax.ShapeDtypeStruct(r.shape, r.dtype) for r in results],
        in_specs=[hbm_any] * 2,
        out_specs=[hbm_any] * 2,
        scratch_shapes=[pltpu.SemaphoreType.DMA((2,))],
    )(*results)


def solution(mesh):
    return jax.shard_map(
        body,
        mesh=mesh,
        in_specs=(
            P("dp", "ctx", None),
            P("dp", "ctx", None),
            P("dp", "ctx", None),
            P(None, "ctx", None, None),
            P(),
        ),
        out_specs=(P("dp", "ctx", None), P(None, "ctx", "dp", None)),
        check_vma=False,
    )
```

```python
import numpy as np
import jax
import jax.numpy as jnp
from jax import lax
from jax.experimental import pallas as pl
from jax.experimental.pallas import tpu as pltpu
from jax.sharding import PartitionSpec as P

M1 = 512
M2 = 128
N = M1 * M2
SMART = 2.0
BF = jnp.bfloat16
F32 = jnp.float32
MESH = pl.DeviceIdType.MESH
NC = 64
ND = 8
GROUP = 2
VMEM_BYTES = 60 * 1024 * 1024


def trig(rows, cols, period):
    turn = (np.arange(rows)[:, None] * np.arange(cols)[None, :]) % period
    angle = turn * (2.0 * np.pi / period)
    return np.cos(angle), np.sin(angle)


def tables():
    c1, s1 = trig(M1, M1, M1)
    tc, ts = trig(M1, M2, N)
    c2, s2 = trig(M2, M2, M2)
    wf = np.block([[c2, s2], [-s2, c2]])
    wi = np.block([[c2, -s2], [s2, c2]])

    def blocks(t):
        return t.reshape(4, 128, M2).transpose(0, 2, 1)

    values = (c1, s1, tc, ts, blocks(tc), blocks(ts), wf, wi)
    kinds = (BF, BF, F32, F32, F32, F32, BF, BF)
    return [jnp.asarray(v.astype(np.float32)).astype(k) for v, k in zip(values, kinds)]


def nn(a, b):
    return lax.dot_general(a, b, (((1,), (0,)), ((), ())), preferred_element_type=F32)


def nt(a, b):
    return lax.dot_general(a, b, (((1,), (1,)), ((), ())), preferred_element_type=F32)


def half(x, j):
    return x[:, j * 128:(j + 1) * 128]


def kernel(emb, per, cot, fil, gain, *refs):
    tabs_h, refs = refs[:8], refs[8:]
    out_h, gout_h = refs[:2]
    (sig, fmsg, oraw, graw) = refs[2:6]
    (rsig, rf, fpiece, filt, x, spec, y, sre, sim, osend, gacc, gsend, grecv, zsend) = refs[6:20]
    (ein, pin, cin, fin, stage, small) = refs[20:26]
    tabs, refs = refs[26:34], refs[34:]
    out, gout, tsem, ssem, rsem = refs
    c1, s1, tc, ts, tct, tst, wf, wi = tabs
    me = lax.axis_index("ctx")
    mine = lax.axis_index("dp")
    inputs = (
        (fil.at[:, :, pl.ds(pl.multiple_of(mine * 32, 32), 32), :], fin),
        (emb.at[0], ein),
        (per.at[0], pin),
        (cot.at[0], cin),
    )
    copies = [pltpu.make_async_copy(h, v, tsem.at[i]) for i, (h, v) in enumerate(inputs)]
    barrier = pltpu.get_barrier_semaphore()

    def peer(a, count, here):
        back = count - a
        step = (back + 1) // 2
        return (here + jnp.where(back % 2 == 1, step, count - step)) & (count - 1)

    def greet(axis, count, here):
        def one(a, _):
            pl.semaphore_signal(
                barrier, inc=1, device_id={axis: (here + a) & (count - 1)}, device_id_type=MESH
            )
            return 0

        for a in range(1, count):
            one(a, 0)

    with jax.named_scope("greet"):
        greet("ctx", NC, me)
        greet("dp", ND, mine)
    for copy in copies:
        copy.start()
    loads = [
        pltpu.make_async_copy(h, v, tsem.at[4 + i]) for i, (h, v) in enumerate(zip(tabs_h, tabs))
    ]
    for load in loads:
        load.start()
    row = lax.broadcasted_iota(jnp.int32, (128, 128), 0)
    col = lax.broadcasted_iota(jnp.int32, (128, 128), 1)
    eye = jnp.where(row == col, 1.0, 0.0).astype(BF)
    picks = [jnp.where(col[:NC] == 2 * row[:NC] + j, 1.0, 0.0).astype(BF) for j in range(2)]

    def pack(i, source):
        for t in range(8):
            stage[:, t, :] = nt(eye, source[t * 128:(t + 1) * 128, :])
        turned = stage[...].astype(BF).reshape(NC, 2, 8, 128)
        for j in range(2):
            sig[i, j] = turned[:, j]

    def scatter(axis, count, here, src, dst, k):
        pltpu.make_async_copy(src(here), dst(here), rsem.at[k]).start()

        def one(a, _):
            to = peer(a, count, here)
            pltpu.make_async_remote_copy(
                src_ref=src(to),
                dst_ref=dst(here),
                send_sem=ssem.at[k],
                recv_sem=rsem.at[k],
                device_id={axis: to},
                device_id_type=MESH,
            ).start()
            return 0

        lax.fori_loop(1, count, one, 0, unroll=7)

    def arrived(ref, k):
        pltpu.make_async_copy(ref, ref, rsem.at[k]).wait()

    def sent(ref, k):
        pltpu.make_async_copy(ref, ref, ssem.at[k]).wait()

    def gone(i, j):
        sent(rsig.at[i, j, pl.ds(0, NC - 1)], 2 * i + j)

    def send(i, j):
        scatter("ctx", NC, me, lambda r: sig.at[i, j, r], lambda r: rsig.at[i, j, r], 2 * i + j)

    with jax.named_scope("pack_filter"):
        copies[0].wait()
        both = jnp.concatenate(picks, 1)
        for i in range(4):
            z = jnp.concatenate(
                [fin[p, i, pl.ds(h, 16, stride=2), :] for h in range(2) for p in range(2)], 0
            ).astype(BF)
            none = jnp.zeros_like(z)
            wide = jnp.concatenate(
                [jnp.concatenate([z, none], 1), jnp.concatenate([none, z], 1)], 0
            )
            small[:, i, :] = nt(both, wide)
        fmsg[...] = small[...].astype(BF)
    with jax.named_scope("pack_embeds"):
        copies[1].wait()
        pack(0, ein)
    with jax.named_scope("greeted"):
        pl.semaphore_wait(barrier, NC + ND - 2)
    with jax.named_scope("send_filter_embeds"):
        scatter("ctx", NC, me, lambda r: fmsg.at[r], lambda r: rf.at[r], 6)
        send(0, 0)
        send(0, 1)
    with jax.named_scope("pack_others"):
        copies[2].wait()
        pin[...] = (ein[...].astype(F32) + pin[...].astype(F32)).astype(BF)
        pack(1, pin)
        copies[3].wait()
        pack(2, cin)
    with jax.named_scope("embeds_sent"):
        gone(0, 0)
    send(1, 0)
    with jax.named_scope("wait_filter"):
        arrived(rf, 6)
    ftab = rf[...].astype(F32).reshape(256, 128)
    for hi in range(2):
        turned = ftab[hi * 128:(hi + 1) * 128].T.astype(BF)
        for j in range(2):
            for h in range(2):
                base = j * 64 + h * 32
                fpiece[2 * h + hi, j] = turned[base:base + 32].reshape(2, 16, 128)
    scatter("dp", ND, mine, lambda d: fpiece, lambda d: filt.at[d], 7)
    with jax.named_scope("embeds_sent_2"):
        gone(0, 1)
    send(1, 1)
    for load in loads:
        load.wait()
    lane = lax.broadcasted_iota(jnp.int32, (1, 128), 1)
    gains = jnp.concatenate(
        [
            jnp.broadcast_to(
                jnp.sum(jnp.where(lane == 2 * me + j, gain[...], 0.0), 1, keepdims=True), (1, 128)
            )
            for j in range(2)
        ],
        1,
    )

    def blocks(step):
        for b in range(4):
            step(b, 0)

    def gather(i, rows16, j):
        return rsig[i, j, rows16].astype(F32).reshape(128, 128)

    def take(i):
        for j in range(2):
            arrived(rsig.at[i, j], 2 * i + j)

        def one(b, _):
            for j in range(2):
                x[i, pl.ds(b * 128, 128), j * 128:(j + 1) * 128] = gather(
                    i, pl.ds(b * 16, 16), j
                ).astype(BF)
            return 0

        blocks(one)

    def forward(i, emit, done=None, js=(0, 1)):
        lanes = slice(js[0] * 128, js[-1] * 128 + 128)

        def one(b, _):
            rows = pl.ds(b * 128, 128)
            a = nn(c1[rows, :], x[i, :, lanes])
            m = nn(s1[rows, :], x[i, :, lanes])
            co, si = tc[rows, :], ts[rows, :]
            for k, j in enumerate(js):
                aj, mj = half(a, k), half(m, k)
                t = jnp.concatenate([aj * co - mj * si, -(mj * co + aj * si)], 1).astype(BF)
                emit(b, j, nt(wf[...], t))
            if done is not None:
                done(b)
            return 0

        blocks(one)

    def keep(i):
        def emit(b, j, value):
            spec[i, j, b] = value

        return emit

    def convolve(i, emit):
        def one(b, _):
            for j in range(2):
                re, im = spec[i, j, b, :128], spec[i, j, b, 128:]
                fr = filt[:, b, j, 0].reshape(128, 128).astype(F32)
                fi = filt[:, b, j, 1].reshape(128, 128).astype(F32)
                prod = jnp.concatenate([fr * re - fi * im, fr * im + fi * re], 0).astype(BF)
                v = nn(wi[...], prod)
                vr, vi = v[:128], v[128:]
                co, si = tct[b], tst[b]
                lanes = pl.ds(pl.multiple_of(b * 128, 128), 128)
                sre[j * 128:(j + 1) * 128, lanes] = (vr * co - vi * si).astype(BF)
                sim[j * 128:(j + 1) * 128, lanes] = (vi * co + vr * si).astype(BF)
            return 0

        blocks(one)

        def two(b, _):
            rows = pl.ds(b * 128, 128)
            conv = (nt(c1[rows, :], sre[...]) - nt(s1[rows, :], sim[...])) * (1.0 / N)
            conv = conv.astype(BF).astype(F32)
            wide = x[i, rows].astype(F32)
            emit(b, rows, wide, wide * conv + gains * wide)
            return 0

        blocks(two)

    def clean(b, rows, wide, value):
        y[rows] = value
        for j in range(2):
            osend[pl.ds(b * 16, 16), j] = half(value, j).reshape(16, 8, 128).astype(BF)

    def shifted(b, rows, wide, value):
        gap = SMART * (value - y[rows])
        y[rows] = gap
        x[2, rows] = (wide * gap).astype(BF)

    def grad_term(err, i, j, b):
        er, ei = err[:128], err[128:]
        re, im = spec[i, j, b, :128], spec[i, j, b, 128:]
        return jnp.concatenate([er * re + ei * im, ei * re - er * im], 0)

    def first(b, j, err):
        gacc[j, b] = grad_term(err, 1, j, b)

    def second(b, j, err):
        g = ((gacc[j, b] + grad_term(err, 0, j, b)) * (1.0 / N)).astype(BF)
        for p in range(2):
            gsend[j, :, b, p] = g[p * 128:(p + 1) * 128].reshape(8, 16, 128)

    def spread(j):
        def done(b):
            if b % GROUP == GROUP - 1:
                rows = pl.ds(b + 1 - GROUP, GROUP)
                scatter(
                    "dp",
                    ND,
                    mine,
                    lambda d: gsend.at[j, d, rows],
                    lambda d: grecv.at[d, j, rows],
                    9 + j,
                )

        return done

    with jax.named_scope("wait_embeds"):
        take(0)
    with jax.named_scope("forward_embeds"):
        forward(0, keep(0))
    with jax.named_scope("shifted_sent"):
        gone(1, 0)
    send(2, 0)
    with jax.named_scope("wait_filter_dp"):
        arrived(filt, 7)
    with jax.named_scope("convolve_embeds"):
        convolve(0, clean)
    with jax.named_scope("shifted_sent_2"):
        gone(1, 1)
    send(2, 1)
    with jax.named_scope("wait_shifted"):
        take(1)
    with jax.named_scope("forward_shifted"):
        forward(1, keep(1))
    with jax.named_scope("convolve_shifted"):
        convolve(1, shifted)
    with jax.named_scope("forward_err_shifted"):
        forward(2, first)
    with jax.named_scope("cotangent_sent"):
        gone(2, 0)
        gone(2, 1)
    with jax.named_scope("send_out"):
        scatter("ctx", NC, me, lambda r: osend.at[r], lambda r: oraw.at[r], 8)

    def errors(j):
        lanes = slice(j * 128, (j + 1) * 128)

        def one(b, _):
            rows = pl.ds(b * 128, 128)
            cot = gather(2, pl.ds(b * 16, 16), j)
            x[2, rows, lanes] = (x[0, rows, lanes].astype(F32) * (cot - y[rows, lanes])).astype(BF)
            return 0

        blocks(one)
        forward(2, second, spread(j), (j,))

    for j in range(2):
        with jax.named_scope("wait_cotangent"):
            arrived(rsig.at[2, j], 4 + j)
        with jax.named_scope("errors"):
            errors(j)
    def pairs(z):
        none = jnp.zeros_like(z)
        wide = jnp.concatenate(
            [jnp.concatenate([z, none], 1), jnp.concatenate([none, z], 1)], 0
        )
        return nt(both, wide)

    for j in range(2):
        with jax.named_scope("wait_terms"):
            arrived(grecv.at[:, j], 9 + j)
        total = grecv[0, j].astype(F32)
        for d in range(1, ND):
            total = total + grecv[d, j].astype(F32)
        for hi in range(2):
            z = jnp.concatenate([total[2 * h + hi].reshape(32, 128) for h in range(2)], 0)
            zsend[j, hi * 32:(hi + 1) * 32] = pairs(z.astype(BF)).reshape(32, 2, 128).astype(BF)
        with jax.named_scope("send_gradient"):
            scatter(
                "ctx", NC, me, lambda r, j=j: zsend.at[j, r], lambda r, j=j: graw.at[j, r], 11 + j
            )
    with jax.named_scope("wait_out"):
        arrived(oraw, 8)
    stage[...] = oraw[...].astype(F32).reshape(128, 8, 128)
    for t in range(8):
        out[0, t * 128:(t + 1) * 128, :] = nt(eye, stage[:, t, :].astype(BF)).astype(BF)
    stores = [
        pltpu.make_async_copy(out, out_h, tsem.at[12]),
        pltpu.make_async_copy(gout, gout_h, tsem.at[13]),
    ]
    stores[0].start()
    with jax.named_scope("wait_gradient"):
        for j in range(2):
            arrived(graw.at[j], 11 + j)
    for i in range(2):
        res = jnp.zeros((128, 128), F32)
        for j in range(2):
            small[:, 2 * j:2 * j + 2, :] = graw[j].astype(F32)
            res = res + nn(small[:, 2 * j + i, :].T.astype(BF), picks[j])
        for k in range(2):
            for h in range(2):
                for p in range(2):
                    base = k * 64 + h * 32 + p * 16
                    gout[p, 2 * i + k, pl.ds(h, 16, stride=2), :] = res[base:base + 16]
    stores[1].start()
    sent(rf.at[pl.ds(0, NC - 1)], 6)
    sent(filt.at[pl.ds(0, ND - 1)], 7)
    sent(osend.at[pl.ds(0, NC - 1)], 8)
    for j in range(2):
        sent(grecv.at[pl.ds(0, ND - 1), j], 9 + j)
        sent(zsend.at[j, pl.ds(0, NC - 1)], 11 + j)
    for copy in stores:
        copy.wait()


def store(clean, grad, clean_out, grad_out, clean_v, grad_v, sem):
    loads = [
        pltpu.make_async_copy(clean, clean_v, sem.at[0]),
        pltpu.make_async_copy(grad, grad_v, sem.at[1]),
    ]
    stores = [
        pltpu.make_async_copy(clean_v, clean_out, sem.at[2]),
        pltpu.make_async_copy(grad_v, grad_out, sem.at[3]),
    ]
    for load in loads:
        load.start()
    for load, out in zip(loads, stores):
        load.wait()
        out.start()
    for out in stores:
        out.wait()


def body(embeds, perturb, cotangent, filter_spectrum, skip_gain):
    tabs = tables()
    vmem = pl.BlockSpec(memory_space=pltpu.VMEM)
    hbm = pl.BlockSpec(memory_space=pltpu.HBM)
    hbm_any = pl.BlockSpec(memory_space=pl.ANY)
    results = pl.pallas_call(
        kernel,
        out_shape=(
            jax.ShapeDtypeStruct((1, 1024, 128), BF),
            jax.ShapeDtypeStruct((2, 4, 32, 128), F32),
        ),
        in_specs=[hbm] * 4 + [vmem] + [hbm] * 8,
        out_specs=(hbm_any, hbm_any),
        scratch_shapes=[
            pltpu.VMEM((3, 2, NC, 8, 128), BF),
            pltpu.VMEM((NC, 4, 128), BF),
            pltpu.VMEM((NC, 2, 8, 128), BF),
            pltpu.VMEM((2, NC, 2, 128), BF),
            pltpu.VMEM((3, 2, NC, 8, 128), BF),
            pltpu.VMEM((NC, 4, 128), BF),
            pltpu.VMEM((4, 2, 2, 16, 128), BF),
            pltpu.VMEM((ND, 4, 2, 2, 16, 128), BF),
            pltpu.VMEM((3, M1, 256), BF),
            pltpu.VMEM((2, 2, 4, 256, 128), F32),
            pltpu.VMEM((M1, 256), F32),
            pltpu.VMEM((256, M1), BF),
            pltpu.VMEM((256, M1), BF),
            pltpu.VMEM((NC, 2, 8, 128), BF),
            pltpu.VMEM((2, 4, 256, 128), F32),
            pltpu.VMEM((2, ND, 4, 2, 16, 128), BF),
            pltpu.VMEM((ND, 2, 4, 2, 16, 128), BF),
            pltpu.VMEM((2, NC, 2, 128), BF),
            pltpu.VMEM((1024, 128), BF),
            pltpu.VMEM((1024, 128), BF),
            pltpu.VMEM((1024, 128), BF),
            pltpu.VMEM((2, 4, 32, 128), F32),
            pltpu.VMEM((128, 8, 128), F32),
            pltpu.VMEM((NC, 4, 128), F32),
        ]
        + [pltpu.VMEM(t.shape, t.dtype) for t in tabs]
        + [
            pltpu.VMEM((1, 1024, 128), BF),
            pltpu.VMEM((2, 4, 32, 128), F32),
            pltpu.SemaphoreType.DMA((14,)),
            pltpu.SemaphoreType.DMA((13,)),
            pltpu.SemaphoreType.DMA((13,)),
        ],
        compiler_params=pltpu.CompilerParams(
            collective_id=0, has_side_effects=True, vmem_limit_bytes=VMEM_BYTES
        ),
    )(embeds, perturb, cotangent, filter_spectrum, skip_gain.reshape(1, 128), *tabs)
    return pl.pallas_call(
        store,
        out_shape=[jax.ShapeDtypeStruct(r.shape, r.dtype) for r in results],
        in_specs=[hbm_any] * 2,
        out_specs=[hbm_any] * 2,
        scratch_shapes=[pltpu.VMEM(r.shape, r.dtype) for r in results]
        + [pltpu.SemaphoreType.DMA((4,))],
    )(*results)


def solution(mesh):
    return jax.shard_map(
        body,
        mesh=mesh,
        in_specs=(
            P("dp", "ctx", None),
            P("dp", "ctx", None),
            P("dp", "ctx", None),
            P(None, "ctx", None, None),
            P(),
        ),
        out_specs=(P("dp", "ctx", None), P(None, "ctx", "dp", None)),
        check_vma=False,
    )
```

```python
import numpy as np
import jax
import jax.numpy as jnp
from jax import lax
from jax.experimental import pallas as pl
from jax.experimental.pallas import tpu as pltpu
from jax.sharding import PartitionSpec as P

M1 = 512
M2 = 128
N = M1 * M2
SMART = 2.0
BF = jnp.bfloat16
F32 = jnp.float32
MESH = pl.DeviceIdType.MESH
NC = 64
ND = 8
GROUP = 2
VMEM_BYTES = 60 * 1024 * 1024


def trig(rows, cols, period):
    turn = (np.arange(rows)[:, None] * np.arange(cols)[None, :]) % period
    angle = turn * (2.0 * np.pi / period)
    return np.cos(angle), np.sin(angle)


def tables():
    c1, s1 = trig(M1, M1, M1)
    tc, ts = trig(M1, M2, N)
    c2, s2 = trig(M2, M2, M2)
    wf = np.block([[c2, s2], [-s2, c2]])
    wi = np.block([[c2, -s2], [s2, c2]])

    def blocks(t):
        return t.reshape(4, 128, M2).transpose(0, 2, 1)

    values = (c1, s1, tc, ts, blocks(tc), blocks(ts), wf, wi)
    kinds = (BF, BF, F32, F32, F32, F32, BF, BF)
    return [jnp.asarray(v.astype(np.float32)).astype(k) for v, k in zip(values, kinds)]


def nn(a, b):
    return lax.dot_general(a, b, (((1,), (0,)), ((), ())), preferred_element_type=F32)


def nt(a, b):
    return lax.dot_general(a, b, (((1,), (1,)), ((), ())), preferred_element_type=F32)


def half(x, j):
    return x[:, j * 128:(j + 1) * 128]


def kernel(emb, per, cot, fil, gain_h, *refs):
    tabs_h, refs = refs[:8], refs[8:]
    out_h, graw = refs[:2]
    (sig, fmsg, oraw) = refs[2:5]
    (rsig, rf, fpiece, filt, x, spec, y, sre, sim, osend, gacc, gsend, grecv, zsend) = refs[5:19]
    (ein, pin, cin, fin, stage, small) = refs[19:25]
    tabs, refs = refs[25:33], refs[33:]
    out, gain, tsem, ssem, rsem = refs
    c1, s1, tc, ts, tct, tst, wf, wi = tabs
    me = lax.axis_index("ctx")
    mine = lax.axis_index("dp")
    inputs = (
        (fil.at[:, :, pl.ds(pl.multiple_of(mine * 32, 32), 32), :], fin),
        (emb.at[0], ein),
        (per.at[0], pin),
        (cot.at[0], cin),
        (gain_h, gain),
    )
    copies = [pltpu.make_async_copy(h, v, tsem.at[i]) for i, (h, v) in enumerate(inputs)]
    barrier = pltpu.get_barrier_semaphore()

    def peer(a, count, here):
        back = count - a
        step = (back + 1) // 2
        return (here + jnp.where(back % 2 == 1, step, count - step)) & (count - 1)

    def greet(axis, count, here):
        def one(a, _):
            pl.semaphore_signal(
                barrier, inc=1, device_id={axis: (here + a) & (count - 1)}, device_id_type=MESH
            )
            return 0

        for a in range(1, count):
            one(a, 0)

    with jax.named_scope("greet"):
        greet("ctx", NC, me)
        greet("dp", ND, mine)
    for copy in copies:
        copy.start()
    loads = [
        pltpu.make_async_copy(h, v, tsem.at[5 + i]) for i, (h, v) in enumerate(zip(tabs_h, tabs))
    ]
    for load in loads:
        load.start()
    row = lax.broadcasted_iota(jnp.int32, (128, 128), 0)
    col = lax.broadcasted_iota(jnp.int32, (128, 128), 1)
    eye = jnp.where(row == col, 1.0, 0.0).astype(BF)
    picks = [jnp.where(col[:NC] == 2 * row[:NC] + j, 1.0, 0.0).astype(BF) for j in range(2)]

    def pack(i, source):
        for t in range(8):
            stage[:, t, :] = nt(eye, source[t * 128:(t + 1) * 128, :])
        turned = stage[...].astype(BF).reshape(NC, 2, 8, 128)
        for j in range(2):
            sig[i, j] = turned[:, j]

    def scatter(axis, count, here, src, dst, k):
        pltpu.make_async_copy(src(here), dst(here), rsem.at[k]).start()

        def one(a, _):
            to = peer(a, count, here)
            pltpu.make_async_remote_copy(
                src_ref=src(to),
                dst_ref=dst(here),
                send_sem=ssem.at[k],
                recv_sem=rsem.at[k],
                device_id={axis: to},
                device_id_type=MESH,
            ).start()
            return 0

        lax.fori_loop(1, count, one, 0, unroll=7)

    def arrived(ref, k):
        pltpu.make_async_copy(ref, ref, rsem.at[k]).wait()

    def sent(ref, k):
        pltpu.make_async_copy(ref, ref, ssem.at[k]).wait()

    def gone(i, j):
        sent(rsig.at[i, j, pl.ds(0, NC - 1)], 2 * i + j)

    def send(i, j):
        scatter("ctx", NC, me, lambda r: sig.at[i, j, r], lambda r: rsig.at[i, j, r], 2 * i + j)

    with jax.named_scope("pack_filter"):
        copies[0].wait()
        both = jnp.concatenate(picks, 1)
        for i in range(4):
            z = jnp.concatenate(
                [fin[p, i, pl.ds(h, 16, stride=2), :] for h in range(2) for p in range(2)], 0
            ).astype(BF)
            none = jnp.zeros_like(z)
            wide = jnp.concatenate(
                [jnp.concatenate([z, none], 1), jnp.concatenate([none, z], 1)], 0
            )
            small[:, i, :] = nt(both, wide)
        fmsg[...] = small[...].astype(BF)
    with jax.named_scope("pack_embeds"):
        copies[1].wait()
        pack(0, ein)
    with jax.named_scope("greeted"):
        pl.semaphore_wait(barrier, NC + ND - 2)
    with jax.named_scope("send_filter_embeds"):
        scatter("ctx", NC, me, lambda r: fmsg.at[r], lambda r: rf.at[r], 6)
        send(0, 0)
        send(0, 1)
    with jax.named_scope("pack_others"):
        copies[2].wait()
        pin[...] = (ein[...].astype(F32) + pin[...].astype(F32)).astype(BF)
        pack(1, pin)
        copies[3].wait()
        pack(2, cin)
    with jax.named_scope("embeds_sent"):
        gone(0, 0)
    send(1, 0)
    with jax.named_scope("wait_filter"):
        arrived(rf, 6)
    ftab = rf[...].astype(F32).reshape(256, 128)
    for hi in range(2):
        turned = ftab[hi * 128:(hi + 1) * 128].T.astype(BF)
        for j in range(2):
            for h in range(2):
                base = j * 64 + h * 32
                fpiece[2 * h + hi, j] = turned[base:base + 32].reshape(2, 16, 128)
    scatter("dp", ND, mine, lambda d: fpiece, lambda d: filt.at[d], 7)
    with jax.named_scope("embeds_sent_2"):
        gone(0, 1)
    send(1, 1)
    copies[4].wait()
    for load in loads:
        load.wait()
    lane = lax.broadcasted_iota(jnp.int32, (1, 128), 1)
    gains = jnp.concatenate(
        [
            jnp.broadcast_to(
                jnp.sum(jnp.where(lane == 2 * me + j, gain[...], 0.0), 1, keepdims=True), (1, 128)
            )
            for j in range(2)
        ],
        1,
    )

    def blocks(step):
        for b in range(4):
            step(b, 0)

    def gather(i, rows16, j):
        return rsig[i, j, rows16].astype(F32).reshape(128, 128)

    def take(i):
        for j in range(2):
            arrived(rsig.at[i, j], 2 * i + j)

        def one(b, _):
            for j in range(2):
                x[i, pl.ds(b * 128, 128), j * 128:(j + 1) * 128] = gather(
                    i, pl.ds(b * 16, 16), j
                ).astype(BF)
            return 0

        blocks(one)

    def forward(i, emit, done=None, js=(0, 1)):
        lanes = slice(js[0] * 128, js[-1] * 128 + 128)

        def one(b, _):
            rows = pl.ds(b * 128, 128)
            a = nn(c1[rows, :], x[i, :, lanes])
            m = nn(s1[rows, :], x[i, :, lanes])
            co, si = tc[rows, :], ts[rows, :]
            for k, j in enumerate(js):
                aj, mj = half(a, k), half(m, k)
                t = jnp.concatenate([aj * co - mj * si, -(mj * co + aj * si)], 1).astype(BF)
                emit(b, j, nt(wf[...], t))
            if done is not None:
                done(b)
            return 0

        blocks(one)

    def keep(i):
        def emit(b, j, value):
            spec[i, j, b] = value

        return emit

    def convolve(i, emit):
        def one(b, _):
            for j in range(2):
                re, im = spec[i, j, b, :128], spec[i, j, b, 128:]
                fr = filt[:, b, j, 0].reshape(128, 128).astype(F32)
                fi = filt[:, b, j, 1].reshape(128, 128).astype(F32)
                prod = jnp.concatenate([fr * re - fi * im, fr * im + fi * re], 0).astype(BF)
                v = nn(wi[...], prod)
                vr, vi = v[:128], v[128:]
                co, si = tct[b], tst[b]
                lanes = pl.ds(pl.multiple_of(b * 128, 128), 128)
                sre[j * 128:(j + 1) * 128, lanes] = (vr * co - vi * si).astype(BF)
                sim[j * 128:(j + 1) * 128, lanes] = (vi * co + vr * si).astype(BF)
            return 0

        blocks(one)

        def two(b, _):
            rows = pl.ds(b * 128, 128)
            conv = (nt(c1[rows, :], sre[...]) - nt(s1[rows, :], sim[...])) * (1.0 / N)
            conv = conv.astype(BF).astype(F32)
            wide = x[i, rows].astype(F32)
            emit(b, rows, wide, wide * conv + gains * wide)
            return 0

        blocks(two)

    def clean(b, rows, wide, value):
        y[rows] = value
        for j in range(2):
            osend[pl.ds(b * 16, 16), j] = half(value, j).reshape(16, 8, 128).astype(BF)

    def shifted(b, rows, wide, value):
        gap = SMART * (value - y[rows])
        y[rows] = gap
        x[2, rows] = (wide * gap).astype(BF)

    def grad_term(err, i, j, b):
        er, ei = err[:128], err[128:]
        re, im = spec[i, j, b, :128], spec[i, j, b, 128:]
        return jnp.concatenate([er * re + ei * im, ei * re - er * im], 0)

    def first(b, j, err):
        gacc[j, b] = grad_term(err, 1, j, b)

    def second(b, j, err):
        g = ((gacc[j, b] + grad_term(err, 0, j, b)) * (1.0 / N)).astype(BF)
        for p in range(2):
            gsend[j, :, b, p] = g[p * 128:(p + 1) * 128].reshape(8, 16, 128)

    def spread(j):
        def done(b):
            if b % GROUP == GROUP - 1:
                rows = pl.ds(b + 1 - GROUP, GROUP)
                scatter(
                    "dp",
                    ND,
                    mine,
                    lambda d: gsend.at[j, d, rows],
                    lambda d: grecv.at[d, j, rows],
                    9 + j,
                )

        return done

    with jax.named_scope("wait_embeds"):
        take(0)
    with jax.named_scope("forward_embeds"):
        forward(0, keep(0))
    with jax.named_scope("shifted_sent"):
        gone(1, 0)
    send(2, 0)
    with jax.named_scope("wait_filter_dp"):
        arrived(filt, 7)
    with jax.named_scope("convolve_embeds"):
        convolve(0, clean)
    with jax.named_scope("shifted_sent_2"):
        gone(1, 1)
    send(2, 1)
    with jax.named_scope("wait_shifted"):
        take(1)
    with jax.named_scope("forward_shifted"):
        forward(1, keep(1))
    with jax.named_scope("convolve_shifted"):
        convolve(1, shifted)
    with jax.named_scope("forward_err_shifted"):
        forward(2, first)
    with jax.named_scope("cotangent_sent"):
        gone(2, 0)
        gone(2, 1)
    with jax.named_scope("send_out"):
        scatter("ctx", NC, me, lambda r: osend.at[r], lambda r: oraw.at[r], 8)

    def errors(j):
        lanes = slice(j * 128, (j + 1) * 128)

        def one(b, _):
            rows = pl.ds(b * 128, 128)
            cot = gather(2, pl.ds(b * 16, 16), j)
            x[2, rows, lanes] = (x[0, rows, lanes].astype(F32) * (cot - y[rows, lanes])).astype(BF)
            return 0

        blocks(one)
        forward(2, second, spread(j), (j,))

    for j in range(2):
        with jax.named_scope("wait_cotangent"):
            arrived(rsig.at[2, j], 4 + j)
        with jax.named_scope("errors"):
            errors(j)
    def pairs(z):
        none = jnp.zeros_like(z)
        wide = jnp.concatenate(
            [jnp.concatenate([z, none], 1), jnp.concatenate([none, z], 1)], 0
        )
        return nt(both, wide)

    for j in range(2):
        with jax.named_scope("wait_terms"):
            arrived(grecv.at[:, j], 9 + j)
        total = grecv[0, j].astype(F32)
        for d in range(1, ND):
            total = total + grecv[d, j].astype(F32)
        for hi in range(2):
            z = jnp.concatenate([total[2 * h + hi].reshape(32, 128) for h in range(2)], 0)
            zsend[j, hi * 32:(hi + 1) * 32] = pairs(z.astype(BF)).reshape(32, 2, 128).astype(BF)
        with jax.named_scope("send_gradient"):
            scatter(
                "ctx", NC, me, lambda r, j=j: zsend.at[j, r], lambda r, j=j: graw.at[j, r], 11 + j
            )
    with jax.named_scope("wait_out"):
        arrived(oraw, 8)
    stage[...] = oraw[...].astype(F32).reshape(128, 8, 128)
    for t in range(8):
        out[0, t * 128:(t + 1) * 128, :] = nt(eye, stage[:, t, :].astype(BF)).astype(BF)
    save = pltpu.make_async_copy(out, out_h, tsem.at[13])
    save.start()
    with jax.named_scope("wait_gradient"):
        for j in range(2):
            arrived(graw.at[j], 11 + j)
    sent(rf.at[pl.ds(0, NC - 1)], 6)
    sent(filt.at[pl.ds(0, ND - 1)], 7)
    sent(osend.at[pl.ds(0, NC - 1)], 8)
    for j in range(2):
        sent(grecv.at[pl.ds(0, ND - 1), j], 9 + j)
        sent(zsend.at[j, pl.ds(0, NC - 1)], 11 + j)
    save.wait()


def store(clean, graw, clean_out, grad_out, clean_v, graw_v, small, grad_v, sem):
    load_clean = pltpu.make_async_copy(clean, clean_v, sem.at[0])
    load_grad = pltpu.make_async_copy(graw, graw_v, sem.at[1])
    save_clean = pltpu.make_async_copy(clean_v, clean_out, sem.at[2])
    save_grad = pltpu.make_async_copy(grad_v, grad_out, sem.at[3])
    load_grad.start()
    load_clean.start()
    row = lax.broadcasted_iota(jnp.int32, (NC, 128), 0)
    col = lax.broadcasted_iota(jnp.int32, (NC, 128), 1)
    picks = [jnp.where(col == 2 * row + j, 1.0, 0.0).astype(BF) for j in range(2)]
    load_grad.wait()
    for j in range(2):
        small[:, 2 * j:2 * j + 2, :] = graw_v[j].astype(F32)
    load_clean.wait()
    save_clean.start()
    for i in range(2):
        res = sum(nn(small[:, 2 * j + i, :].T.astype(BF), picks[j]) for j in range(2))
        for k in range(2):
            for h in range(2):
                for p in range(2):
                    base = k * 64 + h * 32 + p * 16
                    grad_v[p, 2 * i + k, pl.ds(h, 16, stride=2), :] = res[base:base + 16]
    save_grad.start()
    save_clean.wait()
    save_grad.wait()


def body(embeds, perturb, cotangent, filter_spectrum, skip_gain):
    tabs = tables()
    hbm = pl.BlockSpec(memory_space=pltpu.HBM)
    hbm_any = pl.BlockSpec(memory_space=pl.ANY)
    results = pl.pallas_call(
        kernel,
        out_shape=(
            jax.ShapeDtypeStruct((1, 1024, 128), BF),
            jax.ShapeDtypeStruct((2, NC, 2, 128), BF),
        ),
        in_specs=[hbm] * 13,
        out_specs=(hbm_any, hbm_any),
        scratch_shapes=[
            pltpu.VMEM((3, 2, NC, 8, 128), BF),
            pltpu.VMEM((NC, 4, 128), BF),
            pltpu.VMEM((NC, 2, 8, 128), BF),
            pltpu.VMEM((3, 2, NC, 8, 128), BF),
            pltpu.VMEM((NC, 4, 128), BF),
            pltpu.VMEM((4, 2, 2, 16, 128), BF),
            pltpu.VMEM((ND, 4, 2, 2, 16, 128), BF),
            pltpu.VMEM((3, M1, 256), BF),
            pltpu.VMEM((2, 2, 4, 256, 128), F32),
            pltpu.VMEM((M1, 256), F32),
            pltpu.VMEM((256, M1), BF),
            pltpu.VMEM((256, M1), BF),
            pltpu.VMEM((NC, 2, 8, 128), BF),
            pltpu.VMEM((2, 4, 256, 128), F32),
            pltpu.VMEM((2, ND, 4, 2, 16, 128), BF),
            pltpu.VMEM((ND, 2, 4, 2, 16, 128), BF),
            pltpu.VMEM((2, NC, 2, 128), BF),
            pltpu.VMEM((1024, 128), BF),
            pltpu.VMEM((1024, 128), BF),
            pltpu.VMEM((1024, 128), BF),
            pltpu.VMEM((2, 4, 32, 128), F32),
            pltpu.VMEM((128, 8, 128), F32),
            pltpu.VMEM((NC, 4, 128), F32),
        ]
        + [pltpu.VMEM(t.shape, t.dtype) for t in tabs]
        + [
            pltpu.VMEM((1, 1024, 128), BF),
            pltpu.VMEM((1, 128), F32),
            pltpu.SemaphoreType.DMA((14,)),
            pltpu.SemaphoreType.DMA((13,)),
            pltpu.SemaphoreType.DMA((13,)),
        ],
        compiler_params=pltpu.CompilerParams(
            collective_id=0, has_side_effects=True, vmem_limit_bytes=VMEM_BYTES
        ),
    )(embeds, perturb, cotangent, filter_spectrum, skip_gain.reshape(1, 128), *tabs)
    return pl.pallas_call(
        store,
        out_shape=[
            jax.ShapeDtypeStruct((1, 1024, 128), BF),
            jax.ShapeDtypeStruct((2, 4, 32, 128), F32),
        ],
        in_specs=[hbm_any] * 2,
        out_specs=[hbm_any] * 2,
        scratch_shapes=[pltpu.VMEM(r.shape, r.dtype) for r in results]
        + [
            pltpu.VMEM((NC, 4, 128), F32),
            pltpu.VMEM((2, 4, 32, 128), F32),
            pltpu.SemaphoreType.DMA((4,)),
        ],
    )(*results)


def solution(mesh):
    return jax.shard_map(
        body,
        mesh=mesh,
        in_specs=(
            P("dp", "ctx", None),
            P("dp", "ctx", None),
            P("dp", "ctx", None),
            P(None, "ctx", None, None),
            P(),
        ),
        out_specs=(P("dp", "ctx", None), P(None, "ctx", "dp", None)),
        check_vma=False,
    )
```

```python
import numpy as np
import jax
import jax.numpy as jnp
from jax import lax
from jax.experimental import pallas as pl
from jax.experimental.pallas import tpu as pltpu
from jax.sharding import PartitionSpec as P

M1 = 512
M2 = 128
N = M1 * M2
SMART = 2.0
BF = jnp.bfloat16
F32 = jnp.float32
MESH = pl.DeviceIdType.MESH
NC = 64
ND = 8
GROUP = 2
VMEM_BYTES = 60 * 1024 * 1024


def trig(rows, cols, period):
    turn = (np.arange(rows)[:, None] * np.arange(cols)[None, :]) % period
    angle = turn * (2.0 * np.pi / period)
    return np.cos(angle), np.sin(angle)


def tables():
    c1, s1 = trig(M1, M1, M1)
    tc, ts = trig(M1, M2, N)
    c2, s2 = trig(M2, M2, M2)
    wf = np.block([[c2, s2], [-s2, c2]])
    wi = np.block([[c2, -s2], [s2, c2]])

    def blocks(t):
        return t.reshape(4, 128, M2).transpose(0, 2, 1)

    values = (c1, s1, tc, ts, blocks(tc), blocks(ts), wf, wi)
    kinds = (BF, BF, F32, F32, F32, F32, BF, BF)
    return [jnp.asarray(v.astype(np.float32)).astype(k) for v, k in zip(values, kinds)]


def nn(a, b):
    return lax.dot_general(a, b, (((1,), (0,)), ((), ())), preferred_element_type=F32)


def nt(a, b):
    return lax.dot_general(a, b, (((1,), (1,)), ((), ())), preferred_element_type=F32)


def half(x, j):
    return x[:, j * 128:(j + 1) * 128]


def kernel(emb, per, cot, fil, gain_h, *refs):
    tabs_h, refs = refs[:8], refs[8:]
    out_h, graw = refs[:2]
    (sig, fmsg, oraw) = refs[2:5]
    (rsig, rf, fpiece, filt, x, spec, y, sre, sim, osend, gacc, gsend, grecv, zsend) = refs[5:19]
    (ein, pin, cin, fin, stage, small) = refs[19:25]
    tabs, refs = refs[25:33], refs[33:]
    out, gain, tsem, ssem, rsem = refs
    c1, s1, tc, ts, tct, tst, wf, wi = tabs
    me = lax.axis_index("ctx")
    mine = lax.axis_index("dp")
    inputs = (
        (fil.at[:, :, pl.ds(pl.multiple_of(mine * 32, 32), 32), :], fin),
        (emb.at[0], ein),
        (per.at[0], pin),
        (cot.at[0], cin),
        (gain_h, gain),
    )
    copies = [pltpu.make_async_copy(h, v, tsem.at[i]) for i, (h, v) in enumerate(inputs)]
    barrier = pltpu.get_barrier_semaphore()

    def peer(a, count, here):
        back = count - a
        step = (back + 1) // 2
        return (here + jnp.where(back % 2 == 1, step, count - step)) & (count - 1)

    def greet(axis, count, here):
        def one(a, _):
            pl.semaphore_signal(
                barrier, inc=1, device_id={axis: (here + a) & (count - 1)}, device_id_type=MESH
            )
            return 0

        for a in range(1, count):
            one(a, 0)

    with jax.named_scope("greet"):
        greet("ctx", NC, me)
        greet("dp", ND, mine)
    for copy in copies:
        copy.start()
    loads = [
        pltpu.make_async_copy(h, v, tsem.at[5 + i]) for i, (h, v) in enumerate(zip(tabs_h, tabs))
    ]
    for load in loads:
        load.start()
    row = lax.broadcasted_iota(jnp.int32, (128, 128), 0)
    col = lax.broadcasted_iota(jnp.int32, (128, 128), 1)
    eye = jnp.where(row == col, 1.0, 0.0).astype(BF)
    picks = [jnp.where(col[:NC] == 2 * row[:NC] + j, 1.0, 0.0).astype(BF) for j in range(2)]

    def pack(i, source):
        for t in range(8):
            stage[:, t, :] = nt(eye, source[t * 128:(t + 1) * 128, :])
        turned = stage[...].astype(BF).reshape(NC, 2, 8, 128)
        for j in range(2):
            sig[i, j] = turned[:, j]

    def scatter(axis, count, here, src, dst, k):
        pltpu.make_async_copy(src(here), dst(here), rsem.at[k]).start()

        def one(a, _):
            to = peer(a, count, here)
            pltpu.make_async_remote_copy(
                src_ref=src(to),
                dst_ref=dst(here),
                send_sem=ssem.at[k],
                recv_sem=rsem.at[k],
                device_id={axis: to},
                device_id_type=MESH,
            ).start()
            return 0

        lax.fori_loop(1, count, one, 0, unroll=7)

    def arrived(ref, k):
        pltpu.make_async_copy(ref, ref, rsem.at[k]).wait()

    def sent(ref, k):
        pltpu.make_async_copy(ref, ref, ssem.at[k]).wait()

    def gone(i, j):
        sent(rsig.at[i, j, pl.ds(0, NC - 1)], 2 * i + j)

    def send(i, j):
        scatter("ctx", NC, me, lambda r: sig.at[i, j, r], lambda r: rsig.at[i, j, r], 2 * i + j)

    with jax.named_scope("pack_filter"):
        copies[0].wait()
        both = jnp.concatenate(picks, 1)
        for i in range(4):
            z = jnp.concatenate(
                [fin[p, i, pl.ds(h, 16, stride=2), :] for h in range(2) for p in range(2)], 0
            ).astype(BF)
            none = jnp.zeros_like(z)
            wide = jnp.concatenate(
                [jnp.concatenate([z, none], 1), jnp.concatenate([none, z], 1)], 0
            )
            small[:, i, :] = nt(both, wide)
        fmsg[...] = small[...].astype(BF)
    with jax.named_scope("pack_embeds"):
        copies[1].wait()
        pack(0, ein)
    with jax.named_scope("greeted"):
        pl.semaphore_wait(barrier, NC + ND - 2)
    with jax.named_scope("send_filter_embeds"):
        scatter("ctx", NC, me, lambda r: fmsg.at[r], lambda r: rf.at[r], 6)
        send(0, 0)
        send(0, 1)
    with jax.named_scope("pack_others"):
        copies[2].wait()
        pin[...] = (ein[...].astype(F32) + pin[...].astype(F32)).astype(BF)
        pack(1, pin)
        copies[3].wait()
        pack(2, cin)
    with jax.named_scope("embeds_sent"):
        gone(0, 0)
    send(1, 0)
    with jax.named_scope("wait_filter"):
        arrived(rf, 6)
    ftab = rf[...].astype(F32).reshape(256, 128)
    for hi in range(2):
        turned = ftab[hi * 128:(hi + 1) * 128].T.astype(BF)
        for j in range(2):
            for h in range(2):
                base = j * 64 + h * 32
                fpiece[2 * h + hi, j] = turned[base:base + 32].reshape(2, 16, 128)
    scatter("dp", ND, mine, lambda d: fpiece, lambda d: filt.at[d], 7)
    with jax.named_scope("embeds_sent_2"):
        gone(0, 1)
    send(1, 1)
    copies[4].wait()
    for load in loads:
        load.wait()
    lane = lax.broadcasted_iota(jnp.int32, (1, 128), 1)
    gains = jnp.concatenate(
        [
            jnp.broadcast_to(
                jnp.sum(jnp.where(lane == 2 * me + j, gain[...], 0.0), 1, keepdims=True), (1, 128)
            )
            for j in range(2)
        ],
        1,
    )

    def blocks(step):
        for b in range(4):
            step(b, 0)

    def gather(i, rows16, j):
        return rsig[i, j, rows16].astype(F32).reshape(128, 128)

    def take(i):
        for j in range(2):
            arrived(rsig.at[i, j], 2 * i + j)

        def one(b, _):
            for j in range(2):
                x[i, pl.ds(b * 128, 128), j * 128:(j + 1) * 128] = gather(
                    i, pl.ds(b * 16, 16), j
                ).astype(BF)
            return 0

        blocks(one)

    def forward(i, emit, done=None, js=(0, 1)):
        lanes = slice(js[0] * 128, js[-1] * 128 + 128)

        def one(b, _):
            rows = pl.ds(b * 128, 128)
            a = nn(c1[rows, :], x[i, :, lanes])
            m = nn(s1[rows, :], x[i, :, lanes])
            co, si = tc[rows, :], ts[rows, :]
            for k, j in enumerate(js):
                aj, mj = half(a, k), half(m, k)
                t = jnp.concatenate([aj * co - mj * si, -(mj * co + aj * si)], 1).astype(BF)
                emit(b, j, nt(wf[...], t))
            if done is not None:
                done(b)
            return 0

        blocks(one)

    def keep(i):
        def emit(b, j, value):
            spec[i, j, b] = value

        return emit

    def convolve(i, emit):
        def one(b, _):
            for j in range(2):
                re, im = spec[i, j, b, :128], spec[i, j, b, 128:]
                fr = filt[:, b, j, 0].reshape(128, 128).astype(F32)
                fi = filt[:, b, j, 1].reshape(128, 128).astype(F32)
                prod = jnp.concatenate([fr * re - fi * im, fr * im + fi * re], 0).astype(BF)
                v = nn(wi[...], prod)
                vr, vi = v[:128], v[128:]
                co, si = tct[b], tst[b]
                lanes = pl.ds(pl.multiple_of(b * 128, 128), 128)
                sre[j * 128:(j + 1) * 128, lanes] = (vr * co - vi * si).astype(BF)
                sim[j * 128:(j + 1) * 128, lanes] = (vi * co + vr * si).astype(BF)
            return 0

        blocks(one)

        def two(b, _):
            rows = pl.ds(b * 128, 128)
            conv = (nt(c1[rows, :], sre[...]) - nt(s1[rows, :], sim[...])) * (1.0 / N)
            conv = conv.astype(BF).astype(F32)
            wide = x[i, rows].astype(F32)
            emit(b, rows, wide, wide * conv + gains * wide)
            return 0

        blocks(two)

    def clean(b, rows, wide, value):
        y[rows] = value
        for j in range(2):
            osend[pl.ds(b * 16, 16), j] = half(value, j).reshape(16, 8, 128).astype(BF)

    def shifted(b, rows, wide, value):
        gap = SMART * (value - y[rows])
        y[rows] = gap
        x[2, rows] = (wide * gap).astype(BF)

    def grad_term(err, i, j, b):
        er, ei = err[:128], err[128:]
        re, im = spec[i, j, b, :128], spec[i, j, b, 128:]
        return jnp.concatenate([er * re + ei * im, ei * re - er * im], 0)

    def first(b, j, err):
        gacc[j, b] = grad_term(err, 1, j, b)

    def second(b, j, err):
        g = ((gacc[j, b] + grad_term(err, 0, j, b)) * (1.0 / N)).astype(BF)
        for p in range(2):
            gsend[j, :, b, p] = g[p * 128:(p + 1) * 128].reshape(8, 16, 128)

    def spread(j):
        def done(b):
            if b % GROUP == GROUP - 1:
                rows = pl.ds(b + 1 - GROUP, GROUP)
                scatter(
                    "dp",
                    ND,
                    mine,
                    lambda d: gsend.at[j, d, rows],
                    lambda d: grecv.at[d, j, rows],
                    9 + j,
                )

        return done

    with jax.named_scope("wait_embeds"):
        take(0)
    with jax.named_scope("forward_embeds"):
        forward(0, keep(0))
    with jax.named_scope("shifted_sent"):
        gone(1, 0)
    send(2, 0)
    with jax.named_scope("wait_filter_dp"):
        arrived(filt, 7)
    with jax.named_scope("convolve_embeds"):
        convolve(0, clean)
    with jax.named_scope("shifted_sent_2"):
        gone(1, 1)
    send(2, 1)
    with jax.named_scope("wait_shifted"):
        take(1)
    with jax.named_scope("forward_shifted"):
        forward(1, keep(1))
    with jax.named_scope("convolve_shifted"):
        convolve(1, shifted)
    with jax.named_scope("forward_err_shifted"):
        forward(2, first)
    def send_out(j):
        with jax.named_scope("cotangent_sent"):
            gone(2, j)
        with jax.named_scope("send_out"):
            scatter("ctx", NC, me, lambda r: osend.at[r, j], lambda r: oraw.at[r, j], 8 + 5 * j)

    send_out(0)

    def errors(j):
        lanes = slice(j * 128, (j + 1) * 128)

        def one(b, _):
            rows = pl.ds(b * 128, 128)
            cot = gather(2, pl.ds(b * 16, 16), j)
            x[2, rows, lanes] = (x[0, rows, lanes].astype(F32) * (cot - y[rows, lanes])).astype(BF)
            return 0

        blocks(one)
        forward(2, second, spread(j), (j,))

    for j in range(2):
        with jax.named_scope("wait_cotangent"):
            arrived(rsig.at[2, j], 4 + j)
        with jax.named_scope("errors"):
            errors(j)
        if j == 0:
            send_out(1)
    def pairs(z):
        none = jnp.zeros_like(z)
        wide = jnp.concatenate(
            [jnp.concatenate([z, none], 1), jnp.concatenate([none, z], 1)], 0
        )
        return nt(both, wide)

    for j in range(2):
        with jax.named_scope("wait_terms"):
            arrived(grecv.at[:, j], 9 + j)
        total = grecv[0, j].astype(F32)
        for d in range(1, ND):
            total = total + grecv[d, j].astype(F32)
        for hi in range(2):
            z = jnp.concatenate([total[2 * h + hi].reshape(32, 128) for h in range(2)], 0)
            zsend[j, hi * 32:(hi + 1) * 32] = pairs(z.astype(BF)).reshape(32, 2, 128).astype(BF)
        with jax.named_scope("send_gradient"):
            scatter(
                "ctx", NC, me, lambda r, j=j: zsend.at[j, r], lambda r, j=j: graw.at[j, r], 11 + j
            )
    with jax.named_scope("wait_out"):
        for j in range(2):
            arrived(oraw.at[:, j], 8 + 5 * j)
    stage[...] = oraw[...].astype(F32).reshape(128, 8, 128)
    for t in range(8):
        out[0, t * 128:(t + 1) * 128, :] = nt(eye, stage[:, t, :].astype(BF)).astype(BF)
    save = pltpu.make_async_copy(out, out_h, tsem.at[13])
    save.start()
    with jax.named_scope("wait_gradient"):
        for j in range(2):
            arrived(graw.at[j], 11 + j)
    sent(rf.at[pl.ds(0, NC - 1)], 6)
    sent(filt.at[pl.ds(0, ND - 1)], 7)
    for j in range(2):
        sent(osend.at[pl.ds(0, NC - 1), j], 8 + 5 * j)
    for j in range(2):
        sent(grecv.at[pl.ds(0, ND - 1), j], 9 + j)
        sent(zsend.at[j, pl.ds(0, NC - 1)], 11 + j)
    save.wait()


def store(clean, graw, clean_out, grad_out, clean_v, graw_v, small, grad_v, sem):
    load_clean = pltpu.make_async_copy(clean, clean_v, sem.at[0])
    load_grad = pltpu.make_async_copy(graw, graw_v, sem.at[1])
    save_clean = pltpu.make_async_copy(clean_v, clean_out, sem.at[2])
    save_grad = pltpu.make_async_copy(grad_v, grad_out, sem.at[3])
    load_grad.start()
    load_clean.start()
    row = lax.broadcasted_iota(jnp.int32, (NC, 128), 0)
    col = lax.broadcasted_iota(jnp.int32, (NC, 128), 1)
    picks = [jnp.where(col == 2 * row + j, 1.0, 0.0).astype(BF) for j in range(2)]
    load_grad.wait()
    for j in range(2):
        small[:, 2 * j:2 * j + 2, :] = graw_v[j].astype(F32)
    load_clean.wait()
    save_clean.start()
    for i in range(2):
        res = sum(nn(small[:, 2 * j + i, :].T.astype(BF), picks[j]) for j in range(2))
        for k in range(2):
            for h in range(2):
                for p in range(2):
                    base = k * 64 + h * 32 + p * 16
                    grad_v[p, 2 * i + k, pl.ds(h, 16, stride=2), :] = res[base:base + 16]
    save_grad.start()
    save_clean.wait()
    save_grad.wait()


def body(embeds, perturb, cotangent, filter_spectrum, skip_gain):
    tabs = tables()
    hbm = pl.BlockSpec(memory_space=pltpu.HBM)
    hbm_any = pl.BlockSpec(memory_space=pl.ANY)
    results = pl.pallas_call(
        kernel,
        out_shape=(
            jax.ShapeDtypeStruct((1, 1024, 128), BF),
            jax.ShapeDtypeStruct((2, NC, 2, 128), BF),
        ),
        in_specs=[hbm] * 13,
        out_specs=(hbm_any, hbm_any),
        scratch_shapes=[
            pltpu.VMEM((3, 2, NC, 8, 128), BF),
            pltpu.VMEM((NC, 4, 128), BF),
            pltpu.VMEM((NC, 2, 8, 128), BF),
            pltpu.VMEM((3, 2, NC, 8, 128), BF),
            pltpu.VMEM((NC, 4, 128), BF),
            pltpu.VMEM((4, 2, 2, 16, 128), BF),
            pltpu.VMEM((ND, 4, 2, 2, 16, 128), BF),
            pltpu.VMEM((3, M1, 256), BF),
            pltpu.VMEM((2, 2, 4, 256, 128), F32),
            pltpu.VMEM((M1, 256), F32),
            pltpu.VMEM((256, M1), BF),
            pltpu.VMEM((256, M1), BF),
            pltpu.VMEM((NC, 2, 8, 128), BF),
            pltpu.VMEM((2, 4, 256, 128), F32),
            pltpu.VMEM((2, ND, 4, 2, 16, 128), BF),
            pltpu.VMEM((ND, 2, 4, 2, 16, 128), BF),
            pltpu.VMEM((2, NC, 2, 128), BF),
            pltpu.VMEM((1024, 128), BF),
            pltpu.VMEM((1024, 128), BF),
            pltpu.VMEM((1024, 128), BF),
            pltpu.VMEM((2, 4, 32, 128), F32),
            pltpu.VMEM((128, 8, 128), F32),
            pltpu.VMEM((NC, 4, 128), F32),
        ]
        + [pltpu.VMEM(t.shape, t.dtype) for t in tabs]
        + [
            pltpu.VMEM((1, 1024, 128), BF),
            pltpu.VMEM((1, 128), F32),
            pltpu.SemaphoreType.DMA((14,)),
            pltpu.SemaphoreType.DMA((14,)),
            pltpu.SemaphoreType.DMA((14,)),
        ],
        compiler_params=pltpu.CompilerParams(
            collective_id=0, has_side_effects=True, vmem_limit_bytes=VMEM_BYTES
        ),
    )(embeds, perturb, cotangent, filter_spectrum, skip_gain.reshape(1, 128), *tabs)
    return pl.pallas_call(
        store,
        out_shape=[
            jax.ShapeDtypeStruct((1, 1024, 128), BF),
            jax.ShapeDtypeStruct((2, 4, 32, 128), F32),
        ],
        in_specs=[hbm_any] * 2,
        out_specs=[hbm_any] * 2,
        scratch_shapes=[pltpu.VMEM(r.shape, r.dtype) for r in results]
        + [
            pltpu.VMEM((NC, 4, 128), F32),
            pltpu.VMEM((2, 4, 32, 128), F32),
            pltpu.SemaphoreType.DMA((4,)),
        ],
    )(*results)


def solution(mesh):
    return jax.shard_map(
        body,
        mesh=mesh,
        in_specs=(
            P("dp", "ctx", None),
            P("dp", "ctx", None),
            P("dp", "ctx", None),
            P(None, "ctx", None, None),
            P(),
        ),
        out_specs=(P("dp", "ctx", None), P(None, "ctx", "dp", None)),
        check_vma=False,
    )
```
